256 devices in a mesh: wrap: 16 (over x, y_lo, core), normal: 16 (over y_hi, z).
Axes of the slice: x: 4, y: 4 (y_hi: 2, y_lo: 2; y = y_hi * 2 + y_lo), z: 8, core: 2. Of those that a mesh axis runs over, the one named last changes fastest.
Arguments:
- residual: float32 [5, 2, 1024, 2048], P(None, None, 'normal', 'wrap'), may hold values from -144 to 144
- courant_xi: float32 [5, 2, 1024, 2048], P(None, None, 'normal', 'wrap'), may hold values from -300 to 300
- courant_eta: float32 [5, 2, 1024, 2048], P(None, None, 'normal', 'wrap'), may hold values from -300 to 300
- dissip_xi: float32 [2, 1024, 2048], P(None, 'normal', 'wrap'), may hold values from 0.02 to 2
- dissip_eta: float32 [2, 1024, 2048], P(None, 'normal', 'wrap'), may hold values from 0.02 to 2
- coupling: bfloat16 [5, 5, 2, 1024, 2048], P(None, None, None, 'normal', 'wrap'), may hold values from -2.5 to 2.5
Outputs:
- update: float32 [5, 2, 1024, 2048], P(None, None, 'normal', 'wrap')
The draws below stay inside these ranges and needn't reach their ends.
All inputs are finite; a program needn't handle non-finite values.
Results may differ from the reference program's by a relative error of at most 0.0003.
Values sent between devices are 32-bit elements; how exact they have to be, the bound alone decides.
A program may use at most 128 MiB of HBM per device.

```python
import math
import jax
import jax.numpy as jnp
from jax import lax

FIELDS = 5
SPAN = 2
NW = 2048
NN = 1024


def speeds(key):
    line_shape = (FIELDS, SPAN, NN, NW)
    first_key, second_key, third_key = jax.random.split(key, 3)
    lowest = math.log(12.0)
    base = jnp.exp(jax.random.uniform(first_key, (FIELDS, SPAN, 1, 1), jnp.float32, lowest, math.log(300.0)))
    rough = jnp.exp(jax.random.uniform(second_key, line_shape, jnp.float32, math.log(0.5), 0.0))
    sign_part = jnp.where(jax.random.bernoulli(third_key, 0.5, (FIELDS, SPAN, 1, 1)), 1.0, -1.0)
    return jnp.clip(sign_part * base * rough, -300.0, 300.0).astype(jnp.float32)


def draw_courant_xi(key, part):
    return speeds(jax.random.fold_in(key, 11))


def draw_courant_eta(key, part):
    return speeds(jax.random.fold_in(key, 23))


def levels(rng, shape, cuts, low, largest):
    factor_of, own = 1.0, jax.random.fold_in(rng, 6)
    for dim, parts in cuts:
        steps = jnp.exp(jax.random.uniform(jax.random.fold_in(own, dim), (parts,), jnp.float32, low / len(cuts), largest / len(cuts)))
        factor_of = factor_of * jnp.repeat(steps, shape[dim] // parts).reshape([-1 if axis == dim else 1 for axis in range(len(shape))])
    return factor_of


def gaussian(key, dims, width, reach, cuts=(), kind=jnp.bfloat16):
    entries = jax.random.normal(key, dims, jnp.float32) * width
    if len(cuts) > 0:
        entries = levels(key, dims, cuts, -0.22, 0.18) * entries
    return jnp.clip(entries, min=-reach, max=reach).astype(kind)


def setup_inputs(seed: int = 0) -> dict:
    streams_of = jax.random.split(jax.random.key(seed), 7)
    return {
        "residual": gaussian(streams_of[0], (FIELDS, SPAN, NN, NW), 24.0, 144.0, ((2, 16), (3, 16)), jnp.float32),
        "courant_xi": draw_courant_xi(jax.random.fold_in(streams_of[6], 71), 0),
        "courant_eta": draw_courant_eta(jax.random.fold_in(streams_of[6], 71), 0),
        "dissip_xi": jnp.clip(jnp.exp(math.log(2.0) - 4.6051702 * jax.random.uniform(streams_of[3], (SPAN, NN, NW), jnp.float32) ** levels(streams_of[3], (SPAN, NN, NW), ((1, 16), (2, 16)), -0.2, 0.2)), 0.02, 2.0),
        "dissip_eta": jnp.clip(jnp.exp(math.log(2.0) - 4.6051702 * jax.random.uniform(streams_of[4], (SPAN, NN, NW), jnp.float32) ** levels(streams_of[4], (SPAN, NN, NW), ((1, 16), (2, 16)), -0.2, 0.2)), 0.02, 2.0),
        "coupling": gaussian(streams_of[5], (FIELDS, FIELDS, SPAN, NN, NW), FIELDS ** -0.5, 2.5, ((3, 16), (4, 16))),
    }


def block_product(left_block, right_block):
    return jnp.sum(left_block[:, :, None] * right_block[None], axis=1)


def identity(block_width, batch_shape):
    batch_shape = tuple(batch_shape)
    square = jnp.eye(block_width, dtype=jnp.float32).reshape((block_width, block_width) + (1,) * len(batch_shape))
    return jnp.broadcast_to(square, (block_width, block_width) + batch_shape)


def small_solve(matrix, values):
    block_width = matrix.shape[0]
    matrix_rows = [matrix[i] for i in range(block_width)]
    right_sides = [values[i] for i in range(block_width)]
    for column in range(block_width):
        inverse = 1.0 / matrix_rows[column][column]
        matrix_rows[column] = matrix_rows[column] * inverse[None]
        right_sides[column] = right_sides[column] * inverse[None]
        for target in range(block_width):
            if target != column:
                factor = matrix_rows[target][column]
                matrix_rows[target] = matrix_rows[target] - factor[None] * matrix_rows[column]
                right_sides[target] = right_sides[target] - factor[None] * right_sides[column]
    return jnp.stack(right_sides)


def thomas(lower, diag, upper, values):
    block_width = diag.shape[0]
    columns = values.shape[1]
    batch_shape = diag.shape[3:]

    def forward_sweep(scan_carry, row_entries):
        eliminate_previous, substitute_previous = scan_carry
        lower_neighbour, center_block, above, source = row_entries
        pivot_matrix = center_block - block_product(lower_neighbour, eliminate_previous)
        joined = small_solve(pivot_matrix, jnp.concatenate([above, source - block_product(lower_neighbour, substitute_previous)], axis=1))
        outputs = (joined[:, :block_width], joined[:, block_width:])
        return outputs, outputs

    start_state = (jnp.zeros((block_width, block_width) + batch_shape, jnp.float32),
             jnp.zeros((block_width, columns) + batch_shape, jnp.float32))
    input_rows = tuple(jnp.moveaxis(operand, 2, 0) for operand in (lower, diag, upper, values))
    ignored_output, (eliminated_rows, substituted_rows) = lax.scan(forward_sweep, start_state, input_rows)

    def backward(following_value, row_entries):
        eliminate_row, substitute_row = row_entries
        current_row = substitute_row - block_product(eliminate_row, following_value)
        return current_row, current_row

    unused_last, solution = lax.scan(backward, jnp.zeros((block_width, columns) + batch_shape, jnp.float32),
                                     (eliminated_rows, substituted_rows), reverse=True)
    return jnp.moveaxis(solution, 0, 2)


def periodic_solve(lower, diag, upper, values):
    block_width = diag.shape[0]
    row_count = diag.shape[2]
    batch_shape = diag.shape[3:]
    columns = values.shape[1]
    filler = jnp.zeros((block_width, block_width, row_count - 1) + batch_shape, jnp.float32)
    left_cols = jnp.concatenate([-lower[:, :, :1], filler], axis=2)
    right_cols = jnp.concatenate([filler, -upper[:, :, -1:]], axis=2)
    solved = thomas(lower, diag, upper, jnp.concatenate([values, left_cols, right_cols], axis=1))
    base_part = solved[:, :columns]
    last_coef = solved[:, columns:columns + block_width]
    first_coef = solved[:, columns + block_width:]
    corner = jnp.concatenate([
        jnp.concatenate([first_coef[:, :, 0], last_coef[:, :, 0]], axis=1),
        jnp.concatenate([first_coef[:, :, -1], last_coef[:, :, -1]], axis=1)], axis=0)
    corner_values = small_solve(identity(2 * block_width, batch_shape) - corner,
                                jnp.concatenate([base_part[:, :, 0], base_part[:, :, -1]], axis=0))
    return (base_part + block_product(last_coef, corner_values[block_width:][:, :, None])
            + block_product(first_coef, corner_values[:block_width][:, :, None]))


def even_rows(array):
    return array[0::2]


def odd_rows(array):
    return array[1::2]


def pair_system(before, speed, after, damp_before, damping, damp_after, source):
    minus_two = damp_before
    plus_two = damp_after
    minus_one = -2.0 * (damp_before + damping) - 0.25 * (before + speed)
    plus_one = -2.0 * (damping + damp_after) + 0.25 * (speed + after)
    center_block = 1.0 + damp_before + 4.0 * damping + damp_after
    empty = jnp.zeros_like(even_rows(damping))
    lower = jnp.stack([jnp.stack([even_rows(minus_two), even_rows(minus_one)]),
                       jnp.stack([empty, odd_rows(minus_two)])])
    diag = jnp.stack([jnp.stack([even_rows(center_block), even_rows(plus_one)]),
                      jnp.stack([odd_rows(minus_one), odd_rows(center_block)])])
    upper = jnp.stack([jnp.stack([even_rows(plus_two), empty]),
                       jnp.stack([odd_rows(plus_one), odd_rows(plus_two)])])
    values = jnp.stack([even_rows(source), odd_rows(source)])[:, None]
    return lower, diag, upper, values


def unpair(paired):
    cells = paired[:, 0]
    return jnp.moveaxis(cells, 0, 1).reshape((cells.shape[1] * 2,) + cells.shape[2:])


def reference(residual, courant_xi, courant_eta, dissip_xi, dissip_eta, coupling):
    full_shape = residual.shape
    groups = full_shape[0] * full_shape[1]

    def grouped(array):
        return jnp.broadcast_to(array.astype(jnp.float32), full_shape).reshape((groups,) + full_shape[2:])

    def wrap_solve(operands):
        lines = [jnp.transpose(operand) for operand in operands]
        speed = lines[1]
        damping = lines[2]
        lower, diag, upper, values = pair_system(jnp.roll(speed, 1, axis=0), speed, jnp.roll(speed, -1, axis=0),
                                                 jnp.roll(damping, 1, axis=0), damping,
                                                 jnp.roll(damping, -1, axis=0), lines[0])
        return jnp.transpose(unpair(periodic_solve(lower, diag, upper, values)))

    xi_update = lax.map(wrap_solve, (grouped(residual), grouped(courant_xi), grouped(dissip_xi))).reshape(full_shape)
    mixed = coupling[:, 0].astype(jnp.float32) * xi_update[0]
    for source_field in range(1, full_shape[0]):
        mixed = mixed + coupling[:, source_field].astype(jnp.float32) * xi_update[source_field]

    def wall_solve(operands):
        source, speed, damping = operands
        edge = jnp.zeros((1,) + speed.shape[1:], jnp.float32)
        before = jnp.concatenate([edge, speed[:-1]], axis=0)
        after = jnp.concatenate([speed[1:], edge], axis=0)
        damp_before = jnp.concatenate([edge, damping[:-1]], axis=0)
        damp_after = jnp.concatenate([damping[1:], edge], axis=0)
        lower, diag, upper, values = pair_system(before, speed, after, damp_before, damping, damp_after, source)
        return unpair(thomas(lower, diag, upper, values))

    update = lax.map(wall_solve, (grouped(mixed), grouped(courant_eta), grouped(dissip_eta))).reshape(full_shape)
    return update
```

```python
import functools

import jax
import jax.numpy as jnp
from jax import lax
from jax.experimental import pallas as pl
from jax.experimental.pallas import tpu as pltpu
from jax.sharding import PartitionSpec as P

LANES = 128
SUBS = 8


class Stash:
    def __init__(self, ref):
        self.ref, self.used = ref, 0

    def put(self, value):
        rows = value.shape[0]
        start = self.used
        self.used += -(-rows // 8) * 8
        assert self.used <= self.ref.shape[0]
        self.ref[pl.ds(start, rows), :] = value
        return lambda: self.ref[pl.ds(start, rows), :]

    def put_all(self, values):
        return [self.put(value) for value in values]


def fetch(handles):
    return [handle() for handle in handles]


def inverse2(m):
    scale = 1.0 / (m[0] * m[3] - m[1] * m[2])
    return [m[3] * scale, -(m[1] * scale), -(m[2] * scale), m[0] * scale]


def mm(a, b):
    return [
        a[0] * b[0] + a[1] * b[2],
        a[0] * b[1] + a[1] * b[3],
        a[2] * b[0] + a[3] * b[2],
        a[2] * b[1] + a[3] * b[3],
    ]


def mv(a, x):
    return [a[0] * x[0] + a[1] * x[1], a[2] * x[0] + a[3] * x[1]]


def sub(a, b):
    return [p - q for p, q in zip(a, b)]


def add(a, b):
    return [p + q for p, q in zip(a, b)]


def neg(a):
    return [-p for p in a]


def roll(values, shift):
    return [pltpu.roll(v, shift % v.shape[0], 0) for v in values]


def eliminate(cells, speed, damp, spread, source, keep_left, keep_right, stash, keep_rhs_factors):
    b = [damp(j) for j in range(cells)]
    c = [speed(j) for j in range(cells)]
    wide = [spread(v) for v in b]
    off = [spread(-2.0 * (b[j] + b[j + 1])) for j in range(cells - 1)]
    diag = [None] + [spread(1.0 + b[j - 1] + 4.0 * b[j] + b[j + 1]) for j in range(1, cells - 1)]
    diag.append(spread(1.0 + b[cells - 2] + 4.0 * b[cells - 1]))
    edge_l = wide[0] * keep_left
    edge_r = wide[-1] * keep_right
    diag.append(edge_r)
    skew = [0.25 * (c[j] + c[j + 1]) for j in range(cells - 1)]
    above = [off[j] + skew[j] for j in range(cells - 1)]
    below = [off[j] - skew[j] for j in range(cells - 1)]
    skew_l = 0.25 * c[0] * keep_left
    skew_r = 0.25 * c[-1] * keep_right
    above.append(-2.0 * edge_r + skew_r)
    below.append(-2.0 * edge_r - skew_r)
    ll = [edge_l, -2.0 * edge_l + skew_l, -2.0 * edge_l - skew_l, spread(1.0 + 4.0 * b[0] + b[1])]
    e, e_next = [edge_l, below[0]], [None, wide[1]]
    f, f_next = [edge_l, above[0]], [None, wide[1]]
    d, p, q, d_next = diag[1], above[1], below[1], diag[2]
    with_rhs = source is not None
    if with_rhs:
        r = [source(j) for j in range(cells)]
        r_left = [None, r[0]]
        here, after = r[1], r[2]
    saved = []
    for i in range(1, cells - 1):
        t = wide[i + 1] if i < cells - 2 else edge_r
        inv = 1.0 / d
        w1, w2 = inv * p, inv * t
        wl = [inv * e[0], inv * e[1]]
        keep = [w1, w2, wl[0], wl[1]]
        if with_rhs:
            wr = inv * here
            r_left = [-(f[0] * wr) if r_left[0] is None else r_left[0] - f[0] * wr, r_left[1] - f[1] * wr]
            tail = t * wr
            here, after = after - q * wr, (r[i + 2] - tail if i + 2 < cells else -tail)
            keep.append(wr)
        if keep_rhs_factors:
            keep += [inv, q, t, f[0], f[1]]
        saved.append(stash.put_all(keep))
        ll = [ll[0] - f[0] * wl[0], ll[1] - f[0] * wl[1], ll[2] - f[1] * wl[0], ll[3] - f[1] * wl[1]]
        e, e_next = (
            [-(q * wl[a]) if e_next[a] is None else e_next[a] - q * wl[a] for a in (0, 1)],
            [-(t * wl[a]) for a in (0, 1)],
        )
        f, f_next = (
            [-(f[a] * w1) if f_next[a] is None else f_next[a] - f[a] * w1 for a in (0, 1)],
            [-(f[a] * w2) for a in (0, 1)],
        )
        d, p, q, d_next = (
            d_next - q * w1,
            above[i + 1] - q * w2,
            below[i + 1] - t * w1,
            diag[i + 2] - t * w2,
        )
    matrix = ll + [f[0], f_next[0], f[1], f_next[1]] + [e[0], e[1], e_next[0], e_next[1]] + [d, p, q, d_next]
    rhs = r_left + [here, after] if with_rhs else None
    return matrix, rhs, saved


def forward_rhs(cells, source, saved, stash):
    r = [source(j) for j in range(cells)]
    r_left = [None, r[0]]
    here, after = r[1], r[2]
    kept = []
    for i in range(1, cells - 1):
        inv, q, t, f0, f1 = fetch(saved[i - 1][4:9])
        wr = inv * here
        kept.append(stash.put(wr))
        r_left = [-(f0 * wr) if r_left[0] is None else r_left[0] - f0 * wr, r_left[1] - f1 * wr]
        tail = t * wr
        here, after = after - q * wr, (r[i + 2] - tail if i + 2 < cells else -tail)
    return r_left + [here, after], kept


def back(cells, saved, results, joints, write):
    left, right = joints[:2], joints[2:]
    write(0, left[1])
    write(cells - 1, right[0])
    nearer, farther = right[0], right[1]
    for i in range(cells - 2, 0, -1):
        w1, w2, wl0, wl1 = fetch(saved[i - 1][:4])
        value = results[i - 1]() - wl0 * left[0] - wl1 * left[1] - w2 * farther - w1 * nearer
        write(i, value)
        nearer, farther = value, nearer


def merge_matrix(a, b):
    inv = inverse2(add(a[12:16], b[0:4]))
    lm, rm = a[4:8], b[8:12]
    wl, wr = mm(inv, a[8:12]), mm(inv, b[4:8])
    merged = (
        sub(a[0:4], mm(lm, wl)) + neg(mm(lm, wr)) + neg(mm(rm, wl)) + sub(b[12:16], mm(rm, wr))
    )
    return merged, wl + wr + inv + lm + rm


def merge_rhs(a, b, factors):
    inv, lm, rm = factors[8:12], factors[12:16], factors[16:20]
    w = mv(inv, add(a[2:4], b[0:2]))
    return sub(a[0:2], mv(lm, w)) + sub(b[2:4], mv(rm, w)), w


def tree_matrix(parts, stash):
    levels = []
    while len(parts) > 1:
        merged, kept = [], []
        for k in range(0, len(parts), 2):
            m, factors = merge_matrix(parts[k](), parts[k + 1]())
            merged.append(functools.partial(lambda v: v, m))
            kept.append(stash.put_all(factors))
        parts = merged
        levels.append(kept)
    return parts[0](), levels


def tree_rhs(parts, levels, stash):
    kept = []
    for level in levels:
        merged, saved = [], []
        for k, factors in enumerate(level):
            m, w = merge_rhs(parts[2 * k], parts[2 * k + 1], [None] * 8 + fetch(factors[8:20]))
            merged.append(m)
            saved.append(stash.put_all(w))
        parts = merged
        kept.append(saved)
    return parts[0], kept


def tree_back(joints, levels, results):
    spans = [joints]
    for level, saved in zip(reversed(levels), reversed(results)):
        finer = []
        for span, factors, w in zip(spans, level, saved):
            k = fetch(factors[:8])
            middle = sub(sub(fetch(w), mv(k[0:4], span[0:2])), mv(k[4:8], span[2:4]))
            finer.append(span[0:2] + middle)
            finer.append(middle + span[2:4])
        spans = finer
    return spans


def ring_matrix(even, odd, stash):
    before = roll(odd, 1)
    d_even, l_even, u_even = add(even[0:4], before[12:16]), before[8:12], even[4:8]
    d_odd, l_odd, u_odd = add(odd[0:4], even[12:16]), even[8:12], odd[4:8]
    inv = inverse2(d_odd)
    alpha, beta = mm(l_even, roll(inv, 1)), mm(u_even, inv)
    low = neg(mm(alpha, roll(l_odd, 1)))
    high = neg(mm(beta, u_odd))
    mid = sub(sub(d_even, mm(alpha, roll(u_odd, 1))), mm(beta, l_odd))
    factors = [alpha + beta]
    half = d_even[0].shape[0]
    step = 1
    while step < half:
        inv_mid = inverse2(mid)
        alpha = mm(low, roll(inv_mid, step))
        beta = mm(high, roll(inv_mid, -step))
        low_b, low_a = roll(low, step), roll(low, -step)
        high_b, high_a = roll(high, step), roll(high, -step)
        mid = sub(sub(mid, mm(alpha, high_b)), mm(beta, low_a))
        low, high = neg(mm(alpha, low_b)), neg(mm(beta, high_a))
        factors.append(alpha + beta)
        step *= 2
    last = inverse2(add(add(low, mid), high))
    kept = [stash.put_all(level) for level in factors]
    return kept, stash.put_all(last), stash.put_all(mm(inv, l_odd) + mm(inv, u_odd) + inv)


def ring_rhs(even, odd, ring):
    kept, last, outer = ring
    before = roll(odd[2:4], 1)
    f_even, f_odd = add(even[0:2], before), add(odd[0:2], even[2:4])
    k = fetch(kept[0])
    f = sub(sub(f_even, mv(k[0:4], roll(f_odd, 1))), mv(k[4:8], f_odd))
    step = 1
    for level in kept[1:]:
        k = fetch(level)
        f = sub(sub(f, mv(k[0:4], roll(f, step))), mv(k[4:8], roll(f, -step)))
        step *= 2
    x_even = mv(fetch(last), f)
    after = roll(x_even, -1)
    k = fetch(outer)
    x_odd = sub(sub(mv(k[8:12], f_odd), mv(k[0:4], x_even)), mv(k[4:8], after))
    return x_even + x_odd, x_odd + after


def kernel(
    fields, ring_w, ring_n, rows_n,
    residual_hbm, cxi_hbm, ceta_hbm, dxi_hbm, deta_hbm, coupling_hbm,
    out_ref,
    residual, cxi, ceta, dxi, deta, coupling,
    turned_c, turned_r, turned_b, mixed, small_xi, small_eta,
    send_xi, recv_xi, back_send_xi, back_recv_xi,
    send_m, recv_m, send_r, recv_r, back_send_eta, back_recv_eta,
    joints_xi, joints_eta, stash_cells, stash_small, stash_ring,
    in_sems, send_xi_sem, recv_xi_sem, bsend_xi_sem, brecv_xi_sem,
    send_m_sem, recv_m_sem, send_r_sem, recv_r_sem, bsend_eta_sem, brecv_eta_sem,
):
    me_w, me_n = lax.axis_index("wrap"), lax.axis_index("normal")
    lines = 2 * fields
    cells_w, cells_n = LANES // SUBS, rows_n // SUBS
    small = Stash(stash_small)
    cell_store = Stash(stash_cells)

    pairs = [(cxi_hbm, cxi), (dxi_hbm, dxi), (residual_hbm, residual), (ceta_hbm, ceta), (deta_hbm, deta), (coupling_hbm, coupling)]
    loads = [pltpu.make_async_copy(s, t, in_sems.at[i]) for i, (s, t) in enumerate(pairs)]
    for load in loads:
        load.start()

    barrier = pltpu.get_barrier_semaphore()

    def greet(axis, me, size):
        def one(o, carry):
            pl.semaphore_signal(barrier, inc=1, device_id={axis: lax.rem(me + o, size)}, device_id_type=pl.DeviceIdType.MESH)
            return carry

        lax.fori_loop(1, size, one, 0)

    greet("wrap", me_w, ring_w)
    greet("normal", me_n, ring_n)

    send_xi[...] = jnp.zeros_like(send_xi)
    send_r[...] = jnp.zeros_like(send_r)
    back_send_xi[...] = jnp.zeros_like(back_send_xi)
    back_send_eta[...] = jnp.zeros_like(back_send_eta)

    loads[0].wait()
    for f in range(fields):
        turned_c[pl.ds(f * LANES, LANES), :] = cxi[pl.ds(f * LANES, LANES), :].T
    loads[1].wait()
    turned_b[...] = dxi[...].T
    loads[2].wait()
    for f in range(fields):
        turned_r[pl.ds(f * LANES, LANES), :] = residual[pl.ds(f * LANES, LANES), :].T

    def every(ref, count, stride):
        return lambda j: ref[pl.ds(j, count, stride=stride), :]

    def tile(count):
        return lambda v: jnp.concatenate([v] * count, axis=0)

    rows_xi = fields * SUBS
    one_xi = jnp.float32(1.0)
    matrix, rhs, cells_xi = eliminate(
        cells_w, every(turned_c, rows_xi, cells_w), every(turned_b, SUBS, cells_w), tile(fields),
        every(turned_r, rows_xi, cells_w), one_xi, one_xi, cell_store, False,
    )
    for k, v in enumerate(matrix + rhs):
        small_xi[pl.ds(k * rows_xi, rows_xi), :] = v

    def packed(ref, rows, first, count):
        def part(g):
            return lambda: [ref[pl.ds(k * rows + first * SUBS + g, fields, stride=SUBS), :] for k in range(count)]

        return [part(g) for g in range(SUBS)]

    parts = packed(small_xi, rows_xi, 0, 16)
    whole, tree_xi = tree_matrix(parts, small)
    parts_r = [
        [small_xi[pl.ds(k * rows_xi + g, fields, stride=SUBS), :] for k in range(16, 20)] for g in range(SUBS)
    ]
    whole_r, tree_xi_r = tree_rhs(parts_r, tree_xi, small)
    for k, v in enumerate(whole + whole_r):
        send_xi[pl.ds(k, fields, stride=24), :] = v

    pl.semaphore_wait(barrier, ring_w + ring_n - 2)

    def remote(src, dst, send_sem, recv_sem, axis, target):
        return pltpu.make_async_remote_copy(
            src_ref=src, dst_ref=dst, send_sem=send_sem, recv_sem=recv_sem,
            device_id={axis: target}, device_id_type=pl.DeviceIdType.MESH,
        )

    def to_owner(count, size, rows, src, dst, send_sem, recv_sem, axis, me):
        copies = []
        for r in range(count):
            owner = size * r // count
            copy = remote(
                src.at[pl.ds(r * rows, rows), :], dst.at[pl.ds(pl.multiple_of(me * rows, rows), rows), :],
                send_sem.at[r], recv_sem.at[me], axis, owner,
            )

            @pl.when(me != owner)
            def _():
                copy.start()

            @pl.when(me == owner)
            def _():
                dst[pl.ds(owner * rows, rows), :] = src[pl.ds(r * rows, rows), :]

            copies.append((owner, copy))
        return copies

    def owned(count, size, me):
        r = lax.div(me * count + size - 1, size)
        return r, lax.div(r * size, count) == me

    def arrivals(size, rows, dst, recv_sem, axis, me):
        def one(o, carry):
            d = lax.rem(me + o, size)
            slot = dst.at[pl.ds(pl.multiple_of(d * rows, rows), rows), :]
            remote(slot, slot, recv_sem.at[d], recv_sem.at[d], axis, d).wait_recv()
            return carry

        lax.fori_loop(1, size, one, 0)

    def hand_back(r, size, answer, src, dst, send_sem, recv_sem, axis, me):
        for k in range(4):
            src[pl.ds(k, size // 2, stride=16), :] = answer[0][k]
            src[pl.ds(8 + k, size // 2, stride=16), :] = answer[1][k]
        into = dst.at[pl.ds(pl.multiple_of(r * 8, 8), 8), :]

        def one(o, carry):
            d = lax.rem(me + o, size)
            remote(src.at[pl.ds(pl.multiple_of(d * 8, 8), 8), :], into, send_sem.at[d], recv_sem.at[r], axis, d).start()
            return carry

        lax.fori_loop(1, size, one, 0)
        dst[pl.ds(pl.multiple_of(r * 8, 8), 8), :] = src[pl.ds(pl.multiple_of(me * 8, 8), 8), :]

    def wait_back(count, size, dst, recv_sem, axis, me):
        for r in range(count):
            owner = size * r // count
            slot = dst.at[pl.ds(r * 8, 8), :]

            @pl.when(me != owner)
            def _():
                remote(slot, slot, recv_sem.at[r], recv_sem.at[r], axis, owner).wait_recv()

    xi_copies = to_owner(fields, ring_w, 24, send_xi, recv_xi, send_xi_sem, recv_xi_sem, "wrap", me_w)

    loads[3].wait()
    loads[4].wait()
    rows_eta = lines * SUBS
    place = lax.rem(lax.broadcasted_iota(jnp.int32, (rows_eta, LANES), 0), SUBS)
    keep_left = jnp.where((place == 0) & (me_n == 0), 0.0, 1.0).astype(jnp.float32)
    keep_right = jnp.where((place == SUBS - 1) & (me_n == ring_n - 1), 0.0, 1.0).astype(jnp.float32)
    matrix, _, cells_eta = eliminate(
        cells_n, every(ceta, rows_eta, cells_n), every(deta, 2 * SUBS, cells_n), tile(fields),
        None, keep_left, keep_right, cell_store, True,
    )
    for k, v in enumerate(matrix):
        small_eta[pl.ds(k * rows_eta, rows_eta), :] = v

    r_xi, own_xi = owned(fields, ring_w, me_w)

    @pl.when(own_xi)
    def _():
        arrivals(ring_w, 24, recv_xi, recv_xi_sem, "wrap", me_w)
        even = [recv_xi[pl.ds(k, ring_w // 2, stride=48), :] for k in range(20)]
        odd = [recv_xi[pl.ds(24 + k, ring_w // 2, stride=48), :] for k in range(20)]
        ring = ring_matrix(even[:16], odd[:16], Stash(stash_ring))
        answer = ring_rhs(even[16:], odd[16:], ring)
        hand_back(r_xi, ring_w, answer, back_send_xi, back_recv_xi, bsend_xi_sem, brecv_xi_sem, "wrap", me_w)

    trees_eta = []
    for h in range(2):
        whole, tree = tree_matrix(packed(small_eta, rows_eta, h * fields, 16), small)
        for k, v in enumerate(whole):
            send_m[pl.ds(h * fields * 16 + k, fields, stride=16), :] = v
        trees_eta.append(tree)
    m_copies = to_owner(lines, ring_n, 16, send_m, recv_m, send_m_sem, recv_m_sem, "normal", me_n)

    def place_joints(spans, ref, rows, first):
        for g, span in enumerate(spans):
            for k in range(4):
                ref[pl.ds(k * rows + first * SUBS + g, fields, stride=SUBS), :] = span[k]

    wait_back(fields, ring_w, back_recv_xi, brecv_xi_sem, "wrap", me_w)
    joints = [back_recv_xi[pl.ds(k, fields, stride=8), :] for k in range(4)]
    place_joints(tree_back(joints, tree_xi, tree_xi_r), joints_xi, rows_xi, 0)

    def write_xi(j, value):
        turned_r[pl.ds(j, rows_xi, stride=cells_w), :] = value

    back(
        cells_w, cells_xi, [s[4] for s in cells_xi],
        [joints_xi[pl.ds(k * rows_xi, rows_xi), :] for k in range(4)], write_xi,
    )
    for f in range(fields):
        turned_c[pl.ds(f * LANES, LANES), :] = turned_r[pl.ds(f * LANES, LANES), :].T

    loads[5].wait()

    def mix(q, carry):
        start = pl.multiple_of(q * 16, 16)
        xi = [turned_c[pl.ds(j * LANES + start, 16), :] for j in range(fields)]
        for k in range(fields):
            total = None
            for j in range(fields):
                term = coupling[pl.ds((k * fields + j) * LANES + start, 16), :].astype(jnp.float32) * xi[j]
                total = term if total is None else total + term
            mixed[pl.ds(k * LANES + start, 16), :] = total
        return carry

    lax.fori_loop(0, LANES // 16, mix, 0)

    rhs, cells_eta_r = forward_rhs(cells_n, every(mixed, rows_eta, cells_n), cells_eta, cell_store)
    for k, v in enumerate(rhs):
        small_eta[pl.ds(k * rows_eta, rows_eta), :] = v
    trees_eta_r = []
    for h in range(2):
        parts_r = [part() for part in packed(small_eta, rows_eta, h * fields, 4)]
        whole_r, kept = tree_rhs(parts_r, trees_eta[h], small)
        for k, v in enumerate(whole_r):
            send_r[pl.ds(h * fields * 8 + k, fields, stride=8), :] = v
        trees_eta_r.append(kept)
    r_copies = to_owner(lines, ring_n, 8, send_r, recv_r, send_r_sem, recv_r_sem, "normal", me_n)

    r_eta, own_eta = owned(lines, ring_n, me_n)

    @pl.when(own_eta)
    def _():
        arrivals(ring_n, 16, recv_m, recv_m_sem, "normal", me_n)
        even = [recv_m[pl.ds(k, ring_n // 2, stride=32), :] for k in range(16)]
        odd = [recv_m[pl.ds(16 + k, ring_n // 2, stride=32), :] for k in range(16)]
        ring = ring_matrix(even, odd, Stash(stash_ring))
        arrivals(ring_n, 8, recv_r, recv_r_sem, "normal", me_n)
        even = [recv_r[pl.ds(k, ring_n // 2, stride=16), :] for k in range(4)]
        odd = [recv_r[pl.ds(8 + k, ring_n // 2, stride=16), :] for k in range(4)]
        answer = ring_rhs(even, odd, ring)
        hand_back(r_eta, ring_n, answer, back_send_eta, back_recv_eta, bsend_eta_sem, brecv_eta_sem, "normal", me_n)

    wait_back(lines, ring_n, back_recv_eta, brecv_eta_sem, "normal", me_n)
    for h in range(2):
        joints = [back_recv_eta[pl.ds(h * fields * 8 + k, fields, stride=8), :] for k in range(4)]
        place_joints(tree_back(joints, trees_eta[h], trees_eta_r[h]), joints_eta, rows_eta, h * fields)

    def write_eta(j, value):
        out_ref[pl.ds(j, rows_eta, stride=cells_n), :] = value

    back(
        cells_n, cells_eta, cells_eta_r,
        [joints_eta[pl.ds(k * rows_eta, rows_eta), :] for k in range(4)], write_eta,
    )

    for me, copies in ((me_w, xi_copies), (me_n, m_copies), (me_n, r_copies)):
        for owner, copy in copies:

            @pl.when(me != owner)
            def _():
                copy.wait_send()

    def drain(size, src, send_sem, axis, me):
        def one(o, carry):
            d = lax.rem(me + o, size)
            slot = src.at[pl.ds(pl.multiple_of(d * 8, 8), 8), :]
            remote(slot, slot, send_sem.at[d], send_sem.at[d], axis, d).wait_send()
            return carry

        lax.fori_loop(1, size, one, 0)

    @pl.when(own_xi)
    def _():
        drain(ring_w, back_send_xi, bsend_xi_sem, "wrap", me_w)

    @pl.when(own_eta)
    def _():
        drain(ring_n, back_send_eta, bsend_eta_sem, "normal", me_n)


def solution(mesh):
    ring_w, ring_n = mesh.shape["wrap"], mesh.shape["normal"]

    def local(residual, courant_xi, courant_eta, dissip_xi, dissip_eta, coupling):
        fields, _, rows_n, _ = residual.shape
        lines = 2 * fields
        flat = fields * LANES
        cells_w, cells_n = LANES // SUBS, rows_n // SUBS
        xi_rows, eta_rows = fields * SUBS, lines * SUBS
        pad = -(-fields // 8) * 8
        vmem = lambda rows, dtype=jnp.float32: pltpu.VMEM((rows, LANES), dtype)
        dma = lambda count: pltpu.SemaphoreType.DMA((count,))
        scratch = [
            vmem(flat), vmem(flat), vmem(flat), vmem(LANES), vmem(LANES), vmem(fields * flat, jnp.bfloat16),
            vmem(flat), vmem(flat), vmem(LANES), vmem(flat), vmem(20 * xi_rows), vmem(16 * eta_rows),
            vmem(fields * 24), vmem(ring_w * 24), vmem(ring_w * 8), vmem(fields * 8),
            vmem(lines * 16), vmem(ring_n * 16), vmem(lines * 8), vmem(ring_n * 8), vmem(ring_n * 8), vmem(lines * 8),
            vmem(4 * xi_rows), vmem(4 * eta_rows),
            vmem((cells_w - 2) * 5 * xi_rows + (cells_n - 2) * 10 * eta_rows),
            vmem((SUBS - 1) * 22 * 3 * pad),
            vmem((8 * 8 + 4 + 12) * max(8, ring_w // 2, ring_n // 2)),
            dma(6), dma(fields), dma(ring_w), dma(ring_w), dma(fields),
            dma(lines), dma(ring_n), dma(lines), dma(ring_n), dma(ring_n), dma(lines),
        ]
        out = pl.pallas_call(
            functools.partial(kernel, fields, ring_w, ring_n, rows_n),
            out_shape=jax.ShapeDtypeStruct((flat, LANES), jnp.float32),
            in_specs=[pl.BlockSpec(memory_space=pl.ANY)] * 6,
            out_specs=pl.BlockSpec(memory_space=pltpu.VMEM),
            scratch_shapes=scratch,
            compiler_params=pltpu.CompilerParams(
                collective_id=0, has_side_effects=True, vmem_limit_bytes=32 * 1024 * 1024
            ),
        )(
            residual.reshape(flat, LANES), courant_xi.reshape(flat, LANES), courant_eta.reshape(flat, LANES),
            dissip_xi.reshape(LANES, LANES), dissip_eta.reshape(LANES, LANES), coupling.reshape(fields * flat, LANES),
        )
        return out.reshape(residual.shape)

    placed = (
        P(None, None, "normal", "wrap"),
        P(None, None, "normal", "wrap"),
        P(None, None, "normal", "wrap"),
        P(None, "normal", "wrap"),
        P(None, "normal", "wrap"),
        P(None, None, None, "normal", "wrap"),
    )
    return jax.shard_map(
        local, mesh=mesh, in_specs=placed, out_specs=P(None, None, "normal", "wrap"), check_vma=False
    )
```

```python
import functools

import jax
import jax.numpy as jnp
from jax import lax
from jax.experimental import pallas as pl
from jax.experimental.pallas import tpu as pltpu
from jax.sharding import PartitionSpec as P

LANES = 128
SUBS = 8


class Stash:
    def __init__(self, ref):
        self.ref, self.used = ref, 0

    def put(self, value):
        rows = value.shape[0]
        start = self.used
        self.used += -(-rows // 8) * 8
        assert self.used <= self.ref.shape[0]
        self.ref[pl.ds(start, rows), :] = value
        return lambda: self.ref[pl.ds(start, rows), :]

    def put_all(self, values):
        return [self.put(value) for value in values]


def fetch(handles):
    return [handle() for handle in handles]


def inverse2(m):
    scale = 1.0 / (m[0] * m[3] - m[1] * m[2])
    return [m[3] * scale, -(m[1] * scale), -(m[2] * scale), m[0] * scale]


def mm(a, b):
    return [
        a[0] * b[0] + a[1] * b[2],
        a[0] * b[1] + a[1] * b[3],
        a[2] * b[0] + a[3] * b[2],
        a[2] * b[1] + a[3] * b[3],
    ]


def mv(a, x):
    return [a[0] * x[0] + a[1] * x[1], a[2] * x[0] + a[3] * x[1]]


def sub(a, b):
    return [p - q for p, q in zip(a, b)]


def add(a, b):
    return [p + q for p, q in zip(a, b)]


def neg(a):
    return [-p for p in a]


def roll(values, shift):
    return [pltpu.roll(v, shift % v.shape[0], 0) for v in values]


def eliminate(cells, speed, damp, spread, source, keep_left, keep_right, stash, keep_rhs_factors):
    b = [damp(j) for j in range(cells)]
    c = [speed(j) for j in range(cells)]
    wide = [spread(v) for v in b]
    off = [spread(-2.0 * (b[j] + b[j + 1])) for j in range(cells - 1)]
    diag = [None] + [spread(1.0 + b[j - 1] + 4.0 * b[j] + b[j + 1]) for j in range(1, cells - 1)]
    diag.append(spread(1.0 + b[cells - 2] + 4.0 * b[cells - 1]))
    edge_l = wide[0] * keep_left
    edge_r = wide[-1] * keep_right
    diag.append(edge_r)
    skew = [0.25 * (c[j] + c[j + 1]) for j in range(cells - 1)]
    above = [off[j] + skew[j] for j in range(cells - 1)]
    below = [off[j] - skew[j] for j in range(cells - 1)]
    skew_l = 0.25 * c[0] * keep_left
    skew_r = 0.25 * c[-1] * keep_right
    above.append(-2.0 * edge_r + skew_r)
    below.append(-2.0 * edge_r - skew_r)
    ll = [edge_l, -2.0 * edge_l + skew_l, -2.0 * edge_l - skew_l, spread(1.0 + 4.0 * b[0] + b[1])]
    e, e_next = [edge_l, below[0]], [None, wide[1]]
    f, f_next = [edge_l, above[0]], [None, wide[1]]
    d, p, q, d_next = diag[1], above[1], below[1], diag[2]
    with_rhs = source is not None
    if with_rhs:
        r = [source(j) for j in range(cells)]
        r_left = [None, r[0]]
        here, after = r[1], r[2]
    saved = []
    for i in range(1, cells - 1):
        t = wide[i + 1] if i < cells - 2 else edge_r
        inv = 1.0 / d
        w1, w2 = inv * p, inv * t
        wl = [inv * e[0], inv * e[1]]
        keep = [w1, w2, wl[0], wl[1]]
        if with_rhs:
            wr = inv * here
            r_left = [-(f[0] * wr) if r_left[0] is None else r_left[0] - f[0] * wr, r_left[1] - f[1] * wr]
            tail = t * wr
            here, after = after - q * wr, (r[i + 2] - tail if i + 2 < cells else -tail)
            keep.append(wr)
        if keep_rhs_factors:
            keep += [inv, q, t, f[0], f[1]]
        saved.append(stash.put_all(keep))
        ll = [ll[0] - f[0] * wl[0], ll[1] - f[0] * wl[1], ll[2] - f[1] * wl[0], ll[3] - f[1] * wl[1]]
        e, e_next = (
            [-(q * wl[a]) if e_next[a] is None else e_next[a] - q * wl[a] for a in (0, 1)],
            [-(t * wl[a]) for a in (0, 1)],
        )
        f, f_next = (
            [-(f[a] * w1) if f_next[a] is None else f_next[a] - f[a] * w1 for a in (0, 1)],
            [-(f[a] * w2) for a in (0, 1)],
        )
        d, p, q, d_next = (
            d_next - q * w1,
            above[i + 1] - q * w2,
            below[i + 1] - t * w1,
            diag[i + 2] - t * w2,
        )
    matrix = ll + [f[0], f_next[0], f[1], f_next[1]] + [e[0], e[1], e_next[0], e_next[1]] + [d, p, q, d_next]
    rhs = r_left + [here, after] if with_rhs else None
    return matrix, rhs, saved


def forward_rhs(cells, source, saved, stash):
    r = [source(j) for j in range(cells)]
    r_left = [None, r[0]]
    here, after = r[1], r[2]
    kept = []
    for i in range(1, cells - 1):
        inv, q, t, f0, f1 = fetch(saved[i - 1][4:9])
        wr = inv * here
        kept.append(stash.put(wr))
        r_left = [-(f0 * wr) if r_left[0] is None else r_left[0] - f0 * wr, r_left[1] - f1 * wr]
        tail = t * wr
        here, after = after - q * wr, (r[i + 2] - tail if i + 2 < cells else -tail)
    return r_left + [here, after], kept


def back(cells, saved, results, joints, write):
    left, right = joints[:2], joints[2:]
    write(0, left[1])
    write(cells - 1, right[0])
    nearer, farther = right[0], right[1]
    for i in range(cells - 2, 0, -1):
        w1, w2, wl0, wl1 = fetch(saved[i - 1][:4])
        value = results[i - 1]() - wl0 * left[0] - wl1 * left[1] - w2 * farther - w1 * nearer
        write(i, value)
        nearer, farther = value, nearer


def merge_matrix(a, b):
    inv = inverse2(add(a[12:16], b[0:4]))
    lm, rm = a[4:8], b[8:12]
    wl, wr = mm(inv, a[8:12]), mm(inv, b[4:8])
    merged = (
        sub(a[0:4], mm(lm, wl)) + neg(mm(lm, wr)) + neg(mm(rm, wl)) + sub(b[12:16], mm(rm, wr))
    )
    return merged, wl + wr + inv + lm + rm


def merge_rhs(a, b, factors):
    inv, lm, rm = factors[8:12], factors[12:16], factors[16:20]
    w = mv(inv, add(a[2:4], b[0:2]))
    return sub(a[0:2], mv(lm, w)) + sub(b[2:4], mv(rm, w)), w


def tree_matrix(parts, stash):
    levels = []
    while len(parts) > 1:
        merged, kept = [], []
        for k in range(0, len(parts), 2):
            m, factors = merge_matrix(parts[k](), parts[k + 1]())
            merged.append(functools.partial(lambda v: v, m))
            kept.append(stash.put_all(factors))
        parts = merged
        levels.append(kept)
    return parts[0](), levels


def tree_rhs(parts, levels, stash):
    kept = []
    for level in levels:
        merged, saved = [], []
        for k, factors in enumerate(level):
            m, w = merge_rhs(parts[2 * k], parts[2 * k + 1], [None] * 8 + fetch(factors[8:20]))
            merged.append(m)
            saved.append(stash.put_all(w))
        parts = merged
        kept.append(saved)
    return parts[0], kept


def tree_back(joints, levels, results):
    spans = [joints]
    for level, saved in zip(reversed(levels), reversed(results)):
        finer = []
        for span, factors, w in zip(spans, level, saved):
            k = fetch(factors[:8])
            middle = sub(sub(fetch(w), mv(k[0:4], span[0:2])), mv(k[4:8], span[2:4]))
            finer.append(span[0:2] + middle)
            finer.append(middle + span[2:4])
        spans = finer
    return spans


def ring_matrix(even, odd, stash):
    before = roll(odd, 1)
    d_even, l_even, u_even = add(even[0:4], before[12:16]), before[8:12], even[4:8]
    d_odd, l_odd, u_odd = add(odd[0:4], even[12:16]), even[8:12], odd[4:8]
    inv = inverse2(d_odd)
    alpha, beta = mm(l_even, roll(inv, 1)), mm(u_even, inv)
    low = neg(mm(alpha, roll(l_odd, 1)))
    high = neg(mm(beta, u_odd))
    mid = sub(sub(d_even, mm(alpha, roll(u_odd, 1))), mm(beta, l_odd))
    factors = [alpha + beta]
    half = d_even[0].shape[0]
    step = 1
    while step < half:
        inv_mid = inverse2(mid)
        alpha = mm(low, roll(inv_mid, step))
        beta = mm(high, roll(inv_mid, -step))
        low_b, low_a = roll(low, step), roll(low, -step)
        high_b, high_a = roll(high, step), roll(high, -step)
        mid = sub(sub(mid, mm(alpha, high_b)), mm(beta, low_a))
        low, high = neg(mm(alpha, low_b)), neg(mm(beta, high_a))
        factors.append(alpha + beta)
        step *= 2
    last = inverse2(add(add(low, mid), high))
    kept = [stash.put_all(level) for level in factors]
    return kept, stash.put_all(last), stash.put_all(mm(inv, l_odd) + mm(inv, u_odd) + inv)


def ring_rhs(even, odd, ring):
    kept, last, outer = ring
    before = roll(odd[2:4], 1)
    f_even, f_odd = add(even[0:2], before), add(odd[0:2], even[2:4])
    k = fetch(kept[0])
    f = sub(sub(f_even, mv(k[0:4], roll(f_odd, 1))), mv(k[4:8], f_odd))
    step = 1
    for level in kept[1:]:
        k = fetch(level)
        f = sub(sub(f, mv(k[0:4], roll(f, step))), mv(k[4:8], roll(f, -step)))
        step *= 2
    x_even = mv(fetch(last), f)
    after = roll(x_even, -1)
    k = fetch(outer)
    x_odd = sub(sub(mv(k[8:12], f_odd), mv(k[0:4], x_even)), mv(k[4:8], after))
    return x_even + x_odd, x_odd + after


def kernel(
    fields, ring_w, ring_n, rows_n,
    residual_hbm, cxi_hbm, ceta_hbm, dxi_hbm, deta_hbm, coupling_hbm,
    out_ref,
    residual, cxi, ceta, dxi, deta, coupling,
    turned_c, turned_r, turned_b, mixed, small_xi, small_eta,
    send_xi, recv_xi, back_send_xi, back_recv_xi,
    send_m, recv_m, send_r, recv_r, back_send_eta, back_recv_eta,
    joints_xi, joints_eta, stash_cells, stash_small, stash_ring,
    in_sems, send_xi_sem, recv_xi_sem, bsend_xi_sem, brecv_xi_sem,
    send_m_sem, recv_m_sem, send_r_sem, recv_r_sem, bsend_eta_sem, brecv_eta_sem,
):
    me_w, me_n = lax.axis_index("wrap"), lax.axis_index("normal")
    lines = 2 * fields
    cells_w, cells_n = LANES // SUBS, rows_n // SUBS
    small = Stash(stash_small)
    cell_store = Stash(stash_cells)

    pairs = [(cxi_hbm, cxi), (dxi_hbm, dxi), (residual_hbm, residual), (ceta_hbm, ceta), (deta_hbm, deta), (coupling_hbm, coupling)]
    loads = [pltpu.make_async_copy(s, t, in_sems.at[i]) for i, (s, t) in enumerate(pairs)]
    for load in loads:
        load.start()

    barrier = pltpu.get_barrier_semaphore()

    def greet(axis, me, size):
        def one(o, carry):
            pl.semaphore_signal(barrier, inc=1, device_id={axis: lax.rem(me + o, size)}, device_id_type=pl.DeviceIdType.MESH)
            return carry

        lax.fori_loop(1, size, one, 0)

    greet("wrap", me_w, ring_w)
    greet("normal", me_n, ring_n)

    send_xi[...] = jnp.zeros_like(send_xi)
    send_r[...] = jnp.zeros_like(send_r)
    back_send_xi[...] = jnp.zeros_like(back_send_xi)
    back_send_eta[...] = jnp.zeros_like(back_send_eta)

    loads[0].wait()
    for f in range(fields):
        turned_c[pl.ds(f * LANES, LANES), :] = cxi[pl.ds(f * LANES, LANES), :].T
    loads[1].wait()
    turned_b[...] = dxi[...].T
    loads[2].wait()
    for f in range(fields):
        turned_r[pl.ds(f * LANES, LANES), :] = residual[pl.ds(f * LANES, LANES), :].T

    def every(ref, count, stride):
        return lambda j: ref[pl.ds(j, count, stride=stride), :]

    def tile(count):
        return lambda v: jnp.concatenate([v] * count, axis=0)

    rows_xi = fields * SUBS
    one_xi = jnp.float32(1.0)
    matrix, rhs, cells_xi = eliminate(
        cells_w, every(turned_c, rows_xi, cells_w), every(turned_b, SUBS, cells_w), tile(fields),
        every(turned_r, rows_xi, cells_w), one_xi, one_xi, cell_store, False,
    )
    for k, v in enumerate(matrix + rhs):
        small_xi[pl.ds(k * rows_xi, rows_xi), :] = v

    def packed(ref, rows, first, count):
        def part(g):
            return lambda: [ref[pl.ds(k * rows + first * SUBS + g, fields, stride=SUBS), :] for k in range(count)]

        return [part(g) for g in range(SUBS)]

    parts = packed(small_xi, rows_xi, 0, 16)
    whole, tree_xi = tree_matrix(parts, small)
    parts_r = [
        [small_xi[pl.ds(k * rows_xi + g, fields, stride=SUBS), :] for k in range(16, 20)] for g in range(SUBS)
    ]
    whole_r, tree_xi_r = tree_rhs(parts_r, tree_xi, small)
    for k, v in enumerate(whole + whole_r):
        send_xi[pl.ds(k, fields, stride=24), :] = v

    pl.semaphore_wait(barrier, ring_w + ring_n - 2)

    def remote(src, dst, send_sem, recv_sem, axis, target):
        return pltpu.make_async_remote_copy(
            src_ref=src, dst_ref=dst, send_sem=send_sem, recv_sem=recv_sem,
            device_id={axis: target}, device_id_type=pl.DeviceIdType.MESH,
        )

    def to_owner(count, size, rows, src, dst, send_sem, recv_sem, axis, me):
        copies = []
        for r in range(count):
            owner = size * r // count
            copy = remote(
                src.at[pl.ds(r * rows, rows), :], dst.at[pl.ds(pl.multiple_of(me * rows, rows), rows), :],
                send_sem.at[r], recv_sem.at[me], axis, owner,
            )

            @pl.when(me != owner)
            def _():
                copy.start()

            @pl.when(me == owner)
            def _():
                dst[pl.ds(owner * rows, rows), :] = src[pl.ds(r * rows, rows), :]

            copies.append((owner, copy))
        return copies

    def owned(count, size, me):
        r = lax.div(me * count + size - 1, size)
        return r, lax.div(r * size, count) == me

    def arrivals(size, rows, dst, recv_sem, axis, me):
        def one(o, carry):
            d = lax.rem(me + o, size)
            slot = dst.at[pl.ds(pl.multiple_of(d * rows, rows), rows), :]
            remote(slot, slot, recv_sem.at[d], recv_sem.at[d], axis, d).wait_recv()
            return carry

        lax.fori_loop(1, size, one, 0)

    def hand_back(r, size, answer, src, dst, send_sem, recv_sem, axis, me):
        for k in range(4):
            src[pl.ds(k, size // 2, stride=16), :] = answer[0][k]
            src[pl.ds(8 + k, size // 2, stride=16), :] = answer[1][k]
        into = dst.at[pl.ds(pl.multiple_of(r * 8, 8), 8), :]

        def one(o, carry):
            d = lax.rem(me + o, size)
            remote(src.at[pl.ds(pl.multiple_of(d * 8, 8), 8), :], into, send_sem.at[d], recv_sem.at[r], axis, d).start()
            return carry

        lax.fori_loop(1, size, one, 0)
        dst[pl.ds(pl.multiple_of(r * 8, 8), 8), :] = src[pl.ds(pl.multiple_of(me * 8, 8), 8), :]

    def wait_back(count, size, dst, recv_sem, axis, me):
        for r in range(count):
            owner = size * r // count
            slot = dst.at[pl.ds(r * 8, 8), :]

            @pl.when(me != owner)
            def _():
                remote(slot, slot, recv_sem.at[r], recv_sem.at[r], axis, owner).wait_recv()

    xi_copies = to_owner(fields, ring_w, 24, send_xi, recv_xi, send_xi_sem, recv_xi_sem, "wrap", me_w)

    loads[3].wait()
    loads[4].wait()
    rows_eta = lines * SUBS
    place = lax.rem(lax.broadcasted_iota(jnp.int32, (rows_eta, LANES), 0), SUBS)
    keep_left = jnp.where((place == 0) & (me_n == 0), 0.0, 1.0).astype(jnp.float32)
    keep_right = jnp.where((place == SUBS - 1) & (me_n == ring_n - 1), 0.0, 1.0).astype(jnp.float32)
    matrix, _, cells_eta = eliminate(
        cells_n, every(ceta, rows_eta, cells_n), every(deta, 2 * SUBS, cells_n), tile(fields),
        None, keep_left, keep_right, cell_store, True,
    )
    for k, v in enumerate(matrix):
        small_eta[pl.ds(k * rows_eta, rows_eta), :] = v

    r_xi, own_xi = owned(fields, ring_w, me_w)

    @pl.when(own_xi)
    def _():
        arrivals(ring_w, 24, recv_xi, recv_xi_sem, "wrap", me_w)
        even = [recv_xi[pl.ds(k, ring_w // 2, stride=48), :] for k in range(20)]
        odd = [recv_xi[pl.ds(24 + k, ring_w // 2, stride=48), :] for k in range(20)]
        ring = ring_matrix(even[:16], odd[:16], Stash(stash_ring))
        answer = ring_rhs(even[16:], odd[16:], ring)
        hand_back(r_xi, ring_w, answer, back_send_xi, back_recv_xi, bsend_xi_sem, brecv_xi_sem, "wrap", me_w)

    trees_eta = []
    for h in range(2):
        whole, tree = tree_matrix(packed(small_eta, rows_eta, h * fields, 16), small)
        for k, v in enumerate(whole):
            send_m[pl.ds(h * fields * 16 + k, fields, stride=16), :] = v
        trees_eta.append(tree)
    m_copies = to_owner(lines, ring_n, 16, send_m, recv_m, send_m_sem, recv_m_sem, "normal", me_n)

    def place_joints(spans, ref, rows, first):
        for g, span in enumerate(spans):
            for k in range(4):
                ref[pl.ds(k * rows + first * SUBS + g, fields, stride=SUBS), :] = span[k]

    wait_back(fields, ring_w, back_recv_xi, brecv_xi_sem, "wrap", me_w)
    joints = [back_recv_xi[pl.ds(k, fields, stride=8), :] for k in range(4)]
    place_joints(tree_back(joints, tree_xi, tree_xi_r), joints_xi, rows_xi, 0)

    def write_xi(j, value):
        turned_r[pl.ds(j, rows_xi, stride=cells_w), :] = value

    back(
        cells_w, cells_xi, [s[4] for s in cells_xi],
        [joints_xi[pl.ds(k * rows_xi, rows_xi), :] for k in range(4)], write_xi,
    )
    for f in range(fields):
        turned_c[pl.ds(f * LANES, LANES), :] = turned_r[pl.ds(f * LANES, LANES), :].T

    loads[5].wait()

    def mix(q, carry):
        start = pl.multiple_of(q * 16, 16)
        xi = [turned_c[pl.ds(j * LANES + start, 16), :] for j in range(fields)]
        for k in range(fields):
            total = None
            for j in range(fields):
                term = coupling[pl.ds((k * fields + j) * LANES + start, 16), :].astype(jnp.float32) * xi[j]
                total = term if total is None else total + term
            mixed[pl.ds(k * LANES + start, 16), :] = total
        return carry

    lax.fori_loop(0, LANES // 16, mix, 0)

    rhs, cells_eta_r = forward_rhs(cells_n, every(mixed, rows_eta, cells_n), cells_eta, cell_store)
    for k, v in enumerate(rhs):
        small_eta[pl.ds(k * rows_eta, rows_eta), :] = v
    trees_eta_r = []
    for h in range(2):
        parts_r = [part() for part in packed(small_eta, rows_eta, h * fields, 4)]
        whole_r, kept = tree_rhs(parts_r, trees_eta[h], small)
        for k, v in enumerate(whole_r):
            send_r[pl.ds(h * fields * 8 + k, fields, stride=8), :] = v
        trees_eta_r.append(kept)
    r_copies = to_owner(lines, ring_n, 8, send_r, recv_r, send_r_sem, recv_r_sem, "normal", me_n)

    r_eta, own_eta = owned(lines, ring_n, me_n)

    @pl.when(own_eta)
    def _():
        arrivals(ring_n, 16, recv_m, recv_m_sem, "normal", me_n)
        even = [recv_m[pl.ds(k, ring_n // 2, stride=32), :] for k in range(16)]
        odd = [recv_m[pl.ds(16 + k, ring_n // 2, stride=32), :] for k in range(16)]
        ring = ring_matrix(even, odd, Stash(stash_ring))
        arrivals(ring_n, 8, recv_r, recv_r_sem, "normal", me_n)
        even = [recv_r[pl.ds(k, ring_n // 2, stride=16), :] for k in range(4)]
        odd = [recv_r[pl.ds(8 + k, ring_n // 2, stride=16), :] for k in range(4)]
        answer = ring_rhs(even, odd, ring)
        hand_back(r_eta, ring_n, answer, back_send_eta, back_recv_eta, bsend_eta_sem, brecv_eta_sem, "normal", me_n)

    wait_back(lines, ring_n, back_recv_eta, brecv_eta_sem, "normal", me_n)
    for h in range(2):
        joints = [back_recv_eta[pl.ds(h * fields * 8 + k, fields, stride=8), :] for k in range(4)]
        place_joints(tree_back(joints, trees_eta[h], trees_eta_r[h]), joints_eta, rows_eta, h * fields)

    def write_eta(j, value):
        out_ref[pl.ds(j, rows_eta, stride=cells_n), :] = value

    back(
        cells_n, cells_eta, cells_eta_r,
        [joints_eta[pl.ds(k * rows_eta, rows_eta), :] for k in range(4)], write_eta,
    )

    for me, copies in ((me_w, xi_copies), (me_n, m_copies), (me_n, r_copies)):
        for owner, copy in copies:

            @pl.when(me != owner)
            def _():
                copy.wait_send()

    def drain(size, src, send_sem, axis, me):
        def one(o, carry):
            d = lax.rem(me + o, size)
            slot = src.at[pl.ds(pl.multiple_of(d * 8, 8), 8), :]
            remote(slot, slot, send_sem.at[d], send_sem.at[d], axis, d).wait_send()
            return carry

        lax.fori_loop(1, size, one, 0)

    @pl.when(own_xi)
    def _():
        drain(ring_w, back_send_xi, bsend_xi_sem, "wrap", me_w)

    @pl.when(own_eta)
    def _():
        drain(ring_n, back_send_eta, bsend_eta_sem, "normal", me_n)


def solution(mesh):
    ring_w, ring_n = mesh.shape["wrap"], mesh.shape["normal"]

    def local(residual, courant_xi, courant_eta, dissip_xi, dissip_eta, coupling):
        fields, _, rows_n, _ = residual.shape
        lines = 2 * fields
        flat = fields * LANES
        cells_w, cells_n = LANES // SUBS, rows_n // SUBS
        xi_rows, eta_rows = fields * SUBS, lines * SUBS
        pad = -(-fields // 8) * 8
        vmem = lambda rows, dtype=jnp.float32: pltpu.VMEM((rows, LANES), dtype)
        dma = lambda count: pltpu.SemaphoreType.DMA((count,))
        scratch = [
            vmem(flat), vmem(flat), vmem(flat), vmem(LANES), vmem(LANES), vmem(fields * flat, jnp.bfloat16),
            vmem(flat), vmem(flat), vmem(LANES), vmem(flat), vmem(20 * xi_rows), vmem(16 * eta_rows),
            vmem(fields * 24), vmem(ring_w * 24), vmem(ring_w * 8), vmem(fields * 8),
            vmem(lines * 16), vmem(ring_n * 16), vmem(lines * 8), vmem(ring_n * 8), vmem(ring_n * 8), vmem(lines * 8),
            vmem(4 * xi_rows), vmem(4 * eta_rows),
            vmem((cells_w - 2) * 5 * xi_rows + (cells_n - 2) * 10 * eta_rows),
            vmem((SUBS - 1) * 22 * 3 * pad),
            vmem((8 * 8 + 4 + 12) * max(8, ring_w // 2, ring_n // 2)),
            dma(6), dma(fields), dma(ring_w), dma(ring_w), dma(fields),
            dma(lines), dma(ring_n), dma(lines), dma(ring_n), dma(ring_n), dma(lines),
        ]
        out = pl.pallas_call(
            functools.partial(kernel, fields, ring_w, ring_n, rows_n),
            out_shape=jax.ShapeDtypeStruct((flat, LANES), jnp.float32),
            in_specs=[pl.BlockSpec(memory_space=pltpu.HBM)] * 6,
            out_specs=pl.BlockSpec(memory_space=pltpu.VMEM),
            scratch_shapes=scratch,
            compiler_params=pltpu.CompilerParams(
                collective_id=0, has_side_effects=True, vmem_limit_bytes=32 * 1024 * 1024
            ),
        )(
            *[pltpu.with_memory_space_constraint(v, pltpu.HBM) for v in (
            residual.reshape(flat, LANES), courant_xi.reshape(flat, LANES), courant_eta.reshape(flat, LANES),
            dissip_xi.reshape(LANES, LANES), dissip_eta.reshape(LANES, LANES), coupling.reshape(fields * flat, LANES),
            )]
        )
        return out.reshape(residual.shape)

    placed = (
        P(None, None, "normal", "wrap"),
        P(None, None, "normal", "wrap"),
        P(None, None, "normal", "wrap"),
        P(None, "normal", "wrap"),
        P(None, "normal", "wrap"),
        P(None, None, None, "normal", "wrap"),
    )
    return jax.shard_map(
        local, mesh=mesh, in_specs=placed, out_specs=P(None, None, "normal", "wrap"), check_vma=False
    )
```

```python
import functools

import jax
import jax.numpy as jnp
from jax import lax
from jax.experimental import pallas as pl
from jax.experimental.pallas import tpu as pltpu
from jax.sharding import PartitionSpec as P

LANES = 128
SUBS = 8


class Stash:
    def __init__(self, ref):
        self.ref, self.used = ref, 0

    def put(self, value):
        rows = value.shape[0]
        start = self.used
        self.used += -(-rows // 8) * 8
        assert self.used <= self.ref.shape[0]
        self.ref[pl.ds(start, rows), :] = value
        return lambda: self.ref[pl.ds(start, rows), :]

    def put_all(self, values):
        return [self.put(value) for value in values]


def fetch(handles):
    return [handle() for handle in handles]


def inverse2(m):
    scale = 1.0 / (m[0] * m[3] - m[1] * m[2])
    return [m[3] * scale, -(m[1] * scale), -(m[2] * scale), m[0] * scale]


def mm(a, b):
    return [
        a[0] * b[0] + a[1] * b[2],
        a[0] * b[1] + a[1] * b[3],
        a[2] * b[0] + a[3] * b[2],
        a[2] * b[1] + a[3] * b[3],
    ]


def mv(a, x):
    return [a[0] * x[0] + a[1] * x[1], a[2] * x[0] + a[3] * x[1]]


def sub(a, b):
    return [p - q for p, q in zip(a, b)]


def add(a, b):
    return [p + q for p, q in zip(a, b)]


def neg(a):
    return [-p for p in a]


def roll(values, shift):
    return [pltpu.roll(v, shift % v.shape[0], 0) for v in values]


def eliminate(cells, speed, damp, spread, source, keep_left, keep_right, stash, keep_rhs_factors):
    b = [damp(j) for j in range(cells)]
    c = [speed(j) for j in range(cells)]
    wide = [spread(v) for v in b]
    off = [spread(-2.0 * (b[j] + b[j + 1])) for j in range(cells - 1)]
    diag = [None] + [spread(1.0 + b[j - 1] + 4.0 * b[j] + b[j + 1]) for j in range(1, cells - 1)]
    diag.append(spread(1.0 + b[cells - 2] + 4.0 * b[cells - 1]))
    edge_l = wide[0] * keep_left
    edge_r = wide[-1] * keep_right
    diag.append(edge_r)
    skew = [0.25 * (c[j] + c[j + 1]) for j in range(cells - 1)]
    above = [off[j] + skew[j] for j in range(cells - 1)]
    below = [off[j] - skew[j] for j in range(cells - 1)]
    skew_l = 0.25 * c[0] * keep_left
    skew_r = 0.25 * c[-1] * keep_right
    above.append(-2.0 * edge_r + skew_r)
    below.append(-2.0 * edge_r - skew_r)
    ll = [edge_l, -2.0 * edge_l + skew_l, -2.0 * edge_l - skew_l, spread(1.0 + 4.0 * b[0] + b[1])]
    e, e_next = [edge_l, below[0]], [None, wide[1]]
    f, f_next = [edge_l, above[0]], [None, wide[1]]
    d, p, q, d_next = diag[1], above[1], below[1], diag[2]
    with_rhs = source is not None
    if with_rhs:
        r = [source(j) for j in range(cells)]
        r_left = [None, r[0]]
        here, after = r[1], r[2]
    saved = []
    for i in range(1, cells - 1):
        t = wide[i + 1] if i < cells - 2 else edge_r
        inv = 1.0 / d
        w1, w2 = inv * p, inv * t
        wl = [inv * e[0], inv * e[1]]
        keep = [w1, w2, wl[0], wl[1]]
        if with_rhs:
            wr = inv * here
            r_left = [-(f[0] * wr) if r_left[0] is None else r_left[0] - f[0] * wr, r_left[1] - f[1] * wr]
            tail = t * wr
            here, after = after - q * wr, (r[i + 2] - tail if i + 2 < cells else -tail)
            keep.append(wr)
        if keep_rhs_factors:
            keep += [inv, q, t, f[0], f[1]]
        saved.append(stash.put_all(keep))
        ll = [ll[0] - f[0] * wl[0], ll[1] - f[0] * wl[1], ll[2] - f[1] * wl[0], ll[3] - f[1] * wl[1]]
        e, e_next = (
            [-(q * wl[a]) if e_next[a] is None else e_next[a] - q * wl[a] for a in (0, 1)],
            [-(t * wl[a]) for a in (0, 1)],
        )
        f, f_next = (
            [-(f[a] * w1) if f_next[a] is None else f_next[a] - f[a] * w1 for a in (0, 1)],
            [-(f[a] * w2) for a in (0, 1)],
        )
        d, p, q, d_next = (
            d_next - q * w1,
            above[i + 1] - q * w2,
            below[i + 1] - t * w1,
            diag[i + 2] - t * w2,
        )
    matrix = ll + [f[0], f_next[0], f[1], f_next[1]] + [e[0], e[1], e_next[0], e_next[1]] + [d, p, q, d_next]
    rhs = r_left + [here, after] if with_rhs else None
    return matrix, rhs, saved


def forward_rhs(cells, source, saved, stash):
    r = [source(j) for j in range(cells)]
    r_left = [None, r[0]]
    here, after = r[1], r[2]
    kept = []
    for i in range(1, cells - 1):
        inv, q, t, f0, f1 = fetch(saved[i - 1][4:9])
        wr = inv * here
        kept.append(stash.put(wr))
        r_left = [-(f0 * wr) if r_left[0] is None else r_left[0] - f0 * wr, r_left[1] - f1 * wr]
        tail = t * wr
        here, after = after - q * wr, (r[i + 2] - tail if i + 2 < cells else -tail)
    return r_left + [here, after], kept


def back(cells, saved, results, joints, write):
    left, right = joints[:2], joints[2:]
    write(0, left[1])
    write(cells - 1, right[0])
    nearer, farther = right[0], right[1]
    for i in range(cells - 2, 0, -1):
        w1, w2, wl0, wl1 = fetch(saved[i - 1][:4])
        value = results[i - 1]() - wl0 * left[0] - wl1 * left[1] - w2 * farther - w1 * nearer
        write(i, value)
        nearer, farther = value, nearer


def merge_matrix(a, b):
    inv = inverse2(add(a[12:16], b[0:4]))
    lm, rm = a[4:8], b[8:12]
    wl, wr = mm(inv, a[8:12]), mm(inv, b[4:8])
    merged = (
        sub(a[0:4], mm(lm, wl)) + neg(mm(lm, wr)) + neg(mm(rm, wl)) + sub(b[12:16], mm(rm, wr))
    )
    return merged, wl + wr + inv + lm + rm


def merge_rhs(a, b, factors):
    inv, lm, rm = factors[8:12], factors[12:16], factors[16:20]
    w = mv(inv, add(a[2:4], b[0:2]))
    return sub(a[0:2], mv(lm, w)) + sub(b[2:4], mv(rm, w)), w


def tree_matrix(parts, stash):
    levels = []
    while len(parts) > 1:
        merged, kept = [], []
        for k in range(0, len(parts), 2):
            m, factors = merge_matrix(parts[k](), parts[k + 1]())
            merged.append(functools.partial(lambda v: v, m))
            kept.append(stash.put_all(factors))
        parts = merged
        levels.append(kept)
    return parts[0](), levels


def tree_rhs(parts, levels, stash):
    kept = []
    for level in levels:
        merged, saved = [], []
        for k, factors in enumerate(level):
            m, w = merge_rhs(parts[2 * k], parts[2 * k + 1], [None] * 8 + fetch(factors[8:20]))
            merged.append(m)
            saved.append(stash.put_all(w))
        parts = merged
        kept.append(saved)
    return parts[0], kept


def tree_back(joints, levels, results):
    spans = [joints]
    for level, saved in zip(reversed(levels), reversed(results)):
        finer = []
        for span, factors, w in zip(spans, level, saved):
            k = fetch(factors[:8])
            middle = sub(sub(fetch(w), mv(k[0:4], span[0:2])), mv(k[4:8], span[2:4]))
            finer.append(span[0:2] + middle)
            finer.append(middle + span[2:4])
        spans = finer
    return spans


def homes(lines, ring):
    return ring // 2, [spot % (ring // 2) for spot in (0, 1, -1, 2, -2)[: lines // 2]]


def ring_matrix(even, odd, stash):
    before = roll(odd, 1)
    d_even, l_even, u_even = add(even[0:4], before[12:16]), before[8:12], even[4:8]
    d_odd, l_odd, u_odd = add(odd[0:4], even[12:16]), even[8:12], odd[4:8]
    inv = inverse2(d_odd)
    alpha, beta = mm(l_even, roll(inv, 1)), mm(u_even, inv)
    low = neg(mm(alpha, roll(l_odd, 1)))
    high = neg(mm(beta, u_odd))
    mid = sub(sub(d_even, mm(alpha, roll(u_odd, 1))), mm(beta, l_odd))
    factors = [alpha + beta]
    half = d_even[0].shape[0]
    step = 1
    while step < half:
        inv_mid = inverse2(mid)
        alpha = mm(low, roll(inv_mid, step))
        beta = mm(high, roll(inv_mid, -step))
        low_b, low_a = roll(low, step), roll(low, -step)
        high_b, high_a = roll(high, step), roll(high, -step)
        mid = sub(sub(mid, mm(alpha, high_b)), mm(beta, low_a))
        low, high = neg(mm(alpha, low_b)), neg(mm(beta, high_a))
        factors.append(alpha + beta)
        step *= 2
    last = inverse2(add(add(low, mid), high))
    kept = [stash.put_all(level) for level in factors]
    return kept, stash.put_all(last), stash.put_all(mm(inv, l_odd) + mm(inv, u_odd) + inv)


def ring_rhs(even, odd, ring):
    kept, last, outer = ring
    before = roll(odd[2:4], 1)
    f_even, f_odd = add(even[0:2], before), add(odd[0:2], even[2:4])
    k = fetch(kept[0])
    f = sub(sub(f_even, mv(k[0:4], roll(f_odd, 1))), mv(k[4:8], f_odd))
    step = 1
    for level in kept[1:]:
        k = fetch(level)
        f = sub(sub(f, mv(k[0:4], roll(f, step))), mv(k[4:8], roll(f, -step)))
        step *= 2
    x_even = mv(fetch(last), f)
    after = roll(x_even, -1)
    k = fetch(outer)
    x_odd = sub(sub(mv(k[8:12], f_odd), mv(k[0:4], x_even)), mv(k[4:8], after))
    return x_even + x_odd, x_odd + after


def kernel(
    fields, ring_w, ring_n, rows_n,
    residual_hbm, cxi_hbm, ceta_hbm, dxi_hbm, deta_hbm, coupling_hbm,
    out_ref,
    residual, cxi, ceta, dxi, deta, coupling,
    turned_c, turned_r, turned_b, mixed, small_xi, small_eta,
    send_xi, recv_xi, back_send_xi, back_recv_xi,
    send_m, recv_m, send_r, recv_r, back_send_eta, back_recv_eta,
    joints_xi, joints_eta, stash_cells, stash_small, stash_ring,
    in_sems, send_xi_sem, recv_xi_sem, bsend_xi_sem, brecv_xi_sem,
    send_m_sem, recv_m_sem, send_r_sem, recv_r_sem, bsend_eta_sem, brecv_eta_sem,
):
    me_w, me_n = lax.axis_index("wrap"), lax.axis_index("normal")
    lines = 2 * fields
    cells_w, cells_n = LANES // SUBS, rows_n // SUBS
    small = Stash(stash_small)
    cell_store = Stash(stash_cells)

    pairs = [(cxi_hbm, cxi), (dxi_hbm, dxi), (residual_hbm, residual), (ceta_hbm, ceta), (deta_hbm, deta), (coupling_hbm, coupling)]
    loads = [pltpu.make_async_copy(s, t, in_sems.at[i]) for i, (s, t) in enumerate(pairs)]
    for load in loads:
        load.start()

    barrier = pltpu.get_barrier_semaphore()

    def greet(axis, me, size):
        def one(o, carry):
            pl.semaphore_signal(barrier, inc=1, device_id={axis: lax.rem(me + o, size)}, device_id_type=pl.DeviceIdType.MESH)
            return carry

        lax.fori_loop(1, size, one, 0)

    greet("wrap", me_w, ring_w)
    greet("normal", me_n, ring_n)

    send_xi[...] = jnp.zeros_like(send_xi)
    back_send_xi[...] = jnp.zeros_like(back_send_xi)

    loads[0].wait()
    for f in range(fields):
        turned_c[pl.ds(f * LANES, LANES), :] = cxi[pl.ds(f * LANES, LANES), :].T
    loads[1].wait()
    turned_b[...] = dxi[...].T
    loads[2].wait()
    for f in range(fields):
        turned_r[pl.ds(f * LANES, LANES), :] = residual[pl.ds(f * LANES, LANES), :].T

    def every(ref, count, stride):
        return lambda j: ref[pl.ds(j, count, stride=stride), :]

    def tile(count):
        return lambda v: jnp.concatenate([v] * count, axis=0)

    rows_xi = fields * SUBS
    one_xi = jnp.float32(1.0)
    matrix, rhs, cells_xi = eliminate(
        cells_w, every(turned_c, rows_xi, cells_w), every(turned_b, SUBS, cells_w), tile(fields),
        every(turned_r, rows_xi, cells_w), one_xi, one_xi, cell_store, False,
    )
    for k, v in enumerate(matrix + rhs):
        small_xi[pl.ds(k * rows_xi, rows_xi), :] = v

    def packed(ref, rows, first, count):
        def part(g):
            return lambda: [ref[pl.ds(k * rows + first * SUBS + g, fields, stride=SUBS), :] for k in range(count)]

        return [part(g) for g in range(SUBS)]

    parts = packed(small_xi, rows_xi, 0, 16)
    whole, tree_xi = tree_matrix(parts, small)
    parts_r = [
        [small_xi[pl.ds(k * rows_xi + g, fields, stride=SUBS), :] for k in range(16, 20)] for g in range(SUBS)
    ]
    whole_r, tree_xi_r = tree_rhs(parts_r, tree_xi, small)
    for k, v in enumerate(whole + whole_r):
        send_xi[pl.ds(k, fields, stride=24), :] = v

    pl.semaphore_wait(barrier, ring_w + ring_n - 2)

    def remote(src, dst, send_sem, recv_sem, axis, target):
        return pltpu.make_async_remote_copy(
            src_ref=src, dst_ref=dst, send_sem=send_sem, recv_sem=recv_sem,
            device_id={axis: target}, device_id_type=pl.DeviceIdType.MESH,
        )

    def to_owner(count, size, rows, src, dst, send_sem, recv_sem, axis, me):
        copies = []
        for r in range(count):
            owner = size * r // count
            copy = remote(
                src.at[pl.ds(r * rows, rows), :], dst.at[pl.ds(pl.multiple_of(me * rows, rows), rows), :],
                send_sem.at[r], recv_sem.at[me], axis, owner,
            )

            @pl.when(me != owner)
            def _():
                copy.start()

            @pl.when(me == owner)
            def _():
                dst[pl.ds(owner * rows, rows), :] = src[pl.ds(r * rows, rows), :]

            copies.append((owner, copy))
        return copies

    def owned(count, size, me):
        r = lax.div(me * count + size - 1, size)
        return r, lax.div(r * size, count) == me

    def arrivals(size, rows, dst, recv_sem, axis, me):
        def one(o, carry):
            d = lax.rem(me + o, size)
            slot = dst.at[pl.ds(pl.multiple_of(d * rows, rows), rows), :]
            remote(slot, slot, recv_sem.at[d], recv_sem.at[d], axis, d).wait_recv()
            return carry

        lax.fori_loop(1, size, one, 0)

    def hand_back(r, size, answer, src, dst, send_sem, recv_sem, axis, me):
        for k in range(4):
            src[pl.ds(k, size // 2, stride=16), :] = answer[0][k]
            src[pl.ds(8 + k, size // 2, stride=16), :] = answer[1][k]
        into = dst.at[pl.ds(pl.multiple_of(r * 8, 8), 8), :]

        def one(o, carry):
            d = lax.rem(me + o, size)
            remote(src.at[pl.ds(pl.multiple_of(d * 8, 8), 8), :], into, send_sem.at[d], recv_sem.at[r], axis, d).start()
            return carry

        lax.fori_loop(1, size, one, 0)
        dst[pl.ds(pl.multiple_of(r * 8, 8), 8), :] = src[pl.ds(pl.multiple_of(me * 8, 8), 8), :]

    def wait_back(count, size, dst, recv_sem, axis, me):
        for r in range(count):
            owner = size * r // count
            slot = dst.at[pl.ds(r * 8, 8), :]

            @pl.when(me != owner)
            def _():
                remote(slot, slot, recv_sem.at[r], recv_sem.at[r], axis, owner).wait_recv()

    half, sites = homes(lines, ring_n)
    my_half = lax.div(me_n, half)
    my_spot = lax.rem(me_n, half)

    def to_homes(rows, src, dst, send_sem, recv_sem):
        size = 2 * rows
        copies = []
        for side in range(2):
            for j, spot in enumerate(sites):
                target = side * half + spot
                begin = j * size
                copy = remote(
                    src.at[pl.ds(begin, size), :], dst.at[pl.ds(pl.multiple_of(me_n * size, size), size), :],
                    send_sem.at[side * len(sites) + j], recv_sem.at[me_n], "normal", target,
                )

                @pl.when(me_n != target)
                def _():
                    copy.start()

                @pl.when(me_n == target)
                def _():
                    dst[pl.ds(target * size, size), :] = src[pl.ds(begin, size), :]

                copies.append((target, copy))
        return copies

    def home_copy(j, d):
        return remote(
            back_send_eta.at[pl.ds(pl.multiple_of(d * 8, 8), 8), :],
            back_recv_eta.at[pl.ds(j * 8, 8), :],
            bsend_eta_sem.at[lax.rem(d, half)], brecv_eta_sem.at[j], "normal", d,
        )

    xi_copies = to_owner(fields, ring_w, 24, send_xi, recv_xi, send_xi_sem, recv_xi_sem, "wrap", me_w)

    loads[3].wait()
    loads[4].wait()
    rows_eta = lines * SUBS
    place = lax.rem(lax.broadcasted_iota(jnp.int32, (rows_eta, LANES), 0), SUBS)
    keep_left = jnp.where((place == 0) & (me_n == 0), 0.0, 1.0).astype(jnp.float32)
    keep_right = jnp.where((place == SUBS - 1) & (me_n == ring_n - 1), 0.0, 1.0).astype(jnp.float32)
    matrix, _, cells_eta = eliminate(
        cells_n, every(ceta, rows_eta, cells_n), every(deta, 2 * SUBS, cells_n), tile(fields),
        None, keep_left, keep_right, cell_store, True,
    )
    for k, v in enumerate(matrix):
        small_eta[pl.ds(k * rows_eta, rows_eta), :] = v

    r_xi, own_xi = owned(fields, ring_w, me_w)

    @pl.when(own_xi)
    def _():
        arrivals(ring_w, 24, recv_xi, recv_xi_sem, "wrap", me_w)
        even = [recv_xi[pl.ds(k, ring_w // 2, stride=48), :] for k in range(20)]
        odd = [recv_xi[pl.ds(24 + k, ring_w // 2, stride=48), :] for k in range(20)]
        ring = ring_matrix(even[:16], odd[:16], Stash(stash_ring))
        answer = ring_rhs(even[16:], odd[16:], ring)
        hand_back(r_xi, ring_w, answer, back_send_xi, back_recv_xi, bsend_xi_sem, brecv_xi_sem, "wrap", me_w)

    trees_eta = []
    for h in range(2):
        whole, tree = tree_matrix(packed(small_eta, rows_eta, h * fields, 16), small)
        for k, v in enumerate(whole):
            send_m[pl.ds(h * fields * 16 + k, fields, stride=16), :] = v
        trees_eta.append(tree)
    m_copies = to_homes(16, send_m, recv_m, send_m_sem, recv_m_sem)

    def place_joints(spans, ref, rows, first):
        for g, span in enumerate(spans):
            for k in range(4):
                ref[pl.ds(k * rows + first * SUBS + g, fields, stride=SUBS), :] = span[k]

    wait_back(fields, ring_w, back_recv_xi, brecv_xi_sem, "wrap", me_w)
    joints = [back_recv_xi[pl.ds(k, fields, stride=8), :] for k in range(4)]
    place_joints(tree_back(joints, tree_xi, tree_xi_r), joints_xi, rows_xi, 0)

    def write_xi(j, value):
        turned_r[pl.ds(j, rows_xi, stride=cells_w), :] = value

    back(
        cells_w, cells_xi, [s[4] for s in cells_xi],
        [joints_xi[pl.ds(k * rows_xi, rows_xi), :] for k in range(4)], write_xi,
    )
    for f in range(fields):
        turned_c[pl.ds(f * LANES, LANES), :] = turned_r[pl.ds(f * LANES, LANES), :].T

    loads[5].wait()

    def mix(q, carry):
        start = pl.multiple_of(q * 16, 16)
        xi = [turned_c[pl.ds(j * LANES + start, 16), :] for j in range(fields)]
        for k in range(fields):
            total = None
            for j in range(fields):
                term = coupling[pl.ds((k * fields + j) * LANES + start, 16), :].astype(jnp.float32) * xi[j]
                total = term if total is None else total + term
            mixed[pl.ds(k * LANES + start, 16), :] = total
        return carry

    lax.fori_loop(0, LANES // 16, mix, 0)

    rhs, cells_eta_r = forward_rhs(cells_n, every(mixed, rows_eta, cells_n), cells_eta, cell_store)
    for k, v in enumerate(rhs):
        small_eta[pl.ds(k * rows_eta, rows_eta), :] = v
    trees_eta_r = []
    for h in range(2):
        parts_r = [part() for part in packed(small_eta, rows_eta, h * fields, 4)]
        whole_r, kept = tree_rhs(parts_r, trees_eta[h], small)
        for k, v in enumerate(whole_r):
            send_r[pl.ds(h * fields * 4 + k, fields, stride=4), :] = v
        trees_eta_r.append(kept)
    r_copies = to_homes(4, send_r, recv_r, send_r_sem, recv_r_sem)

    own_eta = functools.reduce(lambda a, b: a | b, [my_spot == spot for spot in sites])

    def each_home(act):
        for j, spot in enumerate(sites):

            @pl.when(my_spot == spot)
            def _():
                def one(o, carry):
                    act(home_copy(j, my_half * half + lax.rem(spot + o, half)))
                    return carry

                lax.fori_loop(1, half, one, 0)

    @pl.when(own_eta)
    def _():
        arrivals(ring_n, 32, recv_m, recv_m_sem, "normal", me_n)
        kept = Stash(stash_ring)

        def by_parity(ref, i, rows, count):
            slot = 2 * rows
            return [
                [ref[pl.ds(odd * slot + i * rows + k, ring_n // 2, stride=2 * slot), :] for k in range(count)]
                for odd in range(2)
            ]

        rings = [ring_matrix(*by_parity(recv_m, i, 16, 16), kept) for i in range(2)]
        arrivals(ring_n, 8, recv_r, recv_r_sem, "normal", me_n)
        answers = [ring_rhs(*by_parity(recv_r, i, 4, 4), rings[i]) for i in range(2)]
        for i, answer in enumerate(answers):
            for k in range(4):
                for odd in range(2):
                    back_send_eta[pl.ds(odd * 8 + i * 4 + k, ring_n // 2, stride=16), :] = answer[odd][k]
        each_home(lambda copy: copy.start())
        for j, spot in enumerate(sites):

            @pl.when(my_spot == spot)
            def _():
                back_recv_eta[pl.ds(j * 8, 8), :] = back_send_eta[pl.ds(pl.multiple_of(me_n * 8, 8), 8), :]

    for j, spot in enumerate(sites):

        @pl.when(my_spot != spot)
        def _():
            home_copy(j, my_half * half + spot).wait_recv()

    for h in range(2):
        joints = [back_recv_eta[pl.ds(h * fields * 4 + k, fields, stride=4), :] for k in range(4)]
        place_joints(tree_back(joints, trees_eta[h], trees_eta_r[h]), joints_eta, rows_eta, h * fields)

    def write_eta(j, value):
        out_ref[pl.ds(j, rows_eta, stride=cells_n), :] = value

    back(
        cells_n, cells_eta, cells_eta_r,
        [joints_eta[pl.ds(k * rows_eta, rows_eta), :] for k in range(4)], write_eta,
    )

    for me, copies in ((me_w, xi_copies), (me_n, m_copies), (me_n, r_copies)):
        for owner, copy in copies:

            @pl.when(me != owner)
            def _():
                copy.wait_send()

    def drain(size, src, send_sem, axis, me):
        def one(o, carry):
            d = lax.rem(me + o, size)
            slot = src.at[pl.ds(pl.multiple_of(d * 8, 8), 8), :]
            remote(slot, slot, send_sem.at[d], send_sem.at[d], axis, d).wait_send()
            return carry

        lax.fori_loop(1, size, one, 0)

    @pl.when(own_xi)
    def _():
        drain(ring_w, back_send_xi, bsend_xi_sem, "wrap", me_w)

    @pl.when(own_eta)
    def _():
        each_home(lambda copy: copy.wait_send())


def solution(mesh):
    ring_w, ring_n = mesh.shape["wrap"], mesh.shape["normal"]

    def local(residual, courant_xi, courant_eta, dissip_xi, dissip_eta, coupling):
        fields, _, rows_n, _ = residual.shape
        lines = 2 * fields
        flat = fields * LANES
        cells_w, cells_n = LANES // SUBS, rows_n // SUBS
        xi_rows, eta_rows = fields * SUBS, lines * SUBS
        pad = -(-fields // 8) * 8
        _, sites = homes(lines, ring_n)
        vmem = lambda rows, dtype=jnp.float32: pltpu.VMEM((rows, LANES), dtype)
        dma = lambda count: pltpu.SemaphoreType.DMA((count,))
        scratch = [
            vmem(flat), vmem(flat), vmem(flat), vmem(LANES), vmem(LANES), vmem(fields * flat, jnp.bfloat16),
            vmem(flat), vmem(flat), vmem(LANES), vmem(flat), vmem(20 * xi_rows), vmem(16 * eta_rows),
            vmem(fields * 24), vmem(ring_w * 24), vmem(ring_w * 8), vmem(fields * 8),
            vmem(lines * 16), vmem(ring_n * 32), vmem(lines * 4), vmem(ring_n * 8), vmem(ring_n * 8), vmem(lines * 4),
            vmem(4 * xi_rows), vmem(4 * eta_rows),
            vmem((cells_w - 2) * 5 * xi_rows + (cells_n - 2) * 10 * eta_rows),
            vmem((SUBS - 1) * 22 * 3 * pad),
            vmem(2 * (8 * 8 + 4 + 12) * max(8, ring_w // 2, ring_n // 2)),
            dma(6), dma(fields), dma(ring_w), dma(ring_w), dma(fields),
            dma(2 * len(sites)), dma(ring_n), dma(2 * len(sites)), dma(ring_n), dma(ring_n // 2), dma(len(sites)),
        ]
        out = pl.pallas_call(
            functools.partial(kernel, fields, ring_w, ring_n, rows_n),
            out_shape=jax.ShapeDtypeStruct((flat, LANES), jnp.float32),
            in_specs=[pl.BlockSpec(memory_space=pltpu.HBM)] * 6,
            out_specs=pl.BlockSpec(memory_space=pltpu.VMEM),
            scratch_shapes=scratch,
            compiler_params=pltpu.CompilerParams(
                collective_id=0, has_side_effects=True, vmem_limit_bytes=32 * 1024 * 1024
            ),
        )(
            *[pltpu.with_memory_space_constraint(v, pltpu.HBM) for v in (
            residual.reshape(flat, LANES), courant_xi.reshape(flat, LANES), courant_eta.reshape(flat, LANES),
            dissip_xi.reshape(LANES, LANES), dissip_eta.reshape(LANES, LANES), coupling.reshape(fields * flat, LANES),
            )]
        )
        return out.reshape(residual.shape)

    placed = (
        P(None, None, "normal", "wrap"),
        P(None, None, "normal", "wrap"),
        P(None, None, "normal", "wrap"),
        P(None, "normal", "wrap"),
        P(None, "normal", "wrap"),
        P(None, None, None, "normal", "wrap"),
    )
    return jax.shard_map(
        local, mesh=mesh, in_specs=placed, out_specs=P(None, None, "normal", "wrap"), check_vma=False
    )
```

```python
import functools

import jax
import jax.numpy as jnp
from jax import lax
from jax.experimental import pallas as pl
from jax.experimental.pallas import tpu as pltpu
from jax.sharding import PartitionSpec as P

LANES = 128
SUBS = 8


class Stash:
    def __init__(self, ref):
        self.ref, self.used = ref, 0

    def put(self, value):
        rows = value.shape[0]
        start = self.used
        self.used += -(-rows // 8) * 8
        assert self.used <= self.ref.shape[0]
        self.ref[pl.ds(start, rows), :] = value
        return lambda: self.ref[pl.ds(start, rows), :]

    def put_all(self, values):
        return [self.put(value) for value in values]


def fetch(handles):
    return [handle() for handle in handles]


def inverse2(m):
    scale = 1.0 / (m[0] * m[3] - m[1] * m[2])
    return [m[3] * scale, -(m[1] * scale), -(m[2] * scale), m[0] * scale]


def mm(a, b):
    return [
        a[0] * b[0] + a[1] * b[2],
        a[0] * b[1] + a[1] * b[3],
        a[2] * b[0] + a[3] * b[2],
        a[2] * b[1] + a[3] * b[3],
    ]


def mv(a, x):
    return [a[0] * x[0] + a[1] * x[1], a[2] * x[0] + a[3] * x[1]]


def sub(a, b):
    return [p - q for p, q in zip(a, b)]


def add(a, b):
    return [p + q for p, q in zip(a, b)]


def neg(a):
    return [-p for p in a]


def roll(values, shift):
    return [pltpu.roll(v, shift % v.shape[0], 0) for v in values]


def eliminate(cells, speed, damp, spread, source, keep_left, keep_right, stash, keep_rhs_factors):
    b = [damp(j) for j in range(cells)]
    c = [speed(j) for j in range(cells)]
    wide = [spread(v) for v in b]
    off = [spread(-2.0 * (b[j] + b[j + 1])) for j in range(cells - 1)]
    diag = [None] + [spread(1.0 + b[j - 1] + 4.0 * b[j] + b[j + 1]) for j in range(1, cells - 1)]
    diag.append(spread(1.0 + b[cells - 2] + 4.0 * b[cells - 1]))
    edge_l = wide[0] * keep_left
    edge_r = wide[-1] * keep_right
    diag.append(edge_r)
    skew = [0.25 * (c[j] + c[j + 1]) for j in range(cells - 1)]
    above = [off[j] + skew[j] for j in range(cells - 1)]
    below = [off[j] - skew[j] for j in range(cells - 1)]
    skew_l = 0.25 * c[0] * keep_left
    skew_r = 0.25 * c[-1] * keep_right
    above.append(-2.0 * edge_r + skew_r)
    below.append(-2.0 * edge_r - skew_r)
    ll = [edge_l, -2.0 * edge_l + skew_l, -2.0 * edge_l - skew_l, spread(1.0 + 4.0 * b[0] + b[1])]
    e, e_next = [edge_l, below[0]], [None, wide[1]]
    f, f_next = [edge_l, above[0]], [None, wide[1]]
    d, p, q, d_next = diag[1], above[1], below[1], diag[2]
    with_rhs = source is not None
    if with_rhs:
        r = [source(j) for j in range(cells)]
        r_left = [None, r[0]]
        here, after = r[1], r[2]
    saved = []
    for i in range(1, cells - 1):
        t = wide[i + 1] if i < cells - 2 else edge_r
        inv = 1.0 / d
        w1, w2 = inv * p, inv * t
        wl = [inv * e[0], inv * e[1]]
        keep = [w1, w2, wl[0], wl[1]]
        if with_rhs:
            wr = inv * here
            r_left = [-(f[0] * wr) if r_left[0] is None else r_left[0] - f[0] * wr, r_left[1] - f[1] * wr]
            tail = t * wr
            here, after = after - q * wr, (r[i + 2] - tail if i + 2 < cells else -tail)
            keep.append(wr)
        if keep_rhs_factors:
            keep += [inv, q, t, f[0], f[1]]
        saved.append(stash.put_all(keep))
        ll = [ll[0] - f[0] * wl[0], ll[1] - f[0] * wl[1], ll[2] - f[1] * wl[0], ll[3] - f[1] * wl[1]]
        e, e_next = (
            [-(q * wl[a]) if e_next[a] is None else e_next[a] - q * wl[a] for a in (0, 1)],
            [-(t * wl[a]) for a in (0, 1)],
        )
        f, f_next = (
            [-(f[a] * w1) if f_next[a] is None else f_next[a] - f[a] * w1 for a in (0, 1)],
            [-(f[a] * w2) for a in (0, 1)],
        )
        d, p, q, d_next = (
            d_next - q * w1,
            above[i + 1] - q * w2,
            below[i + 1] - t * w1,
            diag[i + 2] - t * w2,
        )
    matrix = ll + [f[0], f_next[0], f[1], f_next[1]] + [e[0], e[1], e_next[0], e_next[1]] + [d, p, q, d_next]
    rhs = r_left + [here, after] if with_rhs else None
    return matrix, rhs, saved


def forward_rhs(cells, source, saved, stash):
    r = [source(j) for j in range(cells)]
    r_left = [None, r[0]]
    here, after = r[1], r[2]
    kept = []
    for i in range(1, cells - 1):
        inv, q, t, f0, f1 = fetch(saved[i - 1][4:9])
        wr = inv * here
        kept.append(stash.put(wr))
        r_left = [-(f0 * wr) if r_left[0] is None else r_left[0] - f0 * wr, r_left[1] - f1 * wr]
        tail = t * wr
        here, after = after - q * wr, (r[i + 2] - tail if i + 2 < cells else -tail)
    return r_left + [here, after], kept


def back(cells, saved, results, joints, write):
    left, right = joints[:2], joints[2:]
    write(0, left[1])
    write(cells - 1, right[0])
    nearer, farther = right[0], right[1]
    for i in range(cells - 2, 0, -1):
        w1, w2, wl0, wl1 = fetch(saved[i - 1][:4])
        value = results[i - 1]() - wl0 * left[0] - wl1 * left[1] - w2 * farther - w1 * nearer
        write(i, value)
        nearer, farther = value, nearer


def merge_matrix(a, b):
    inv = inverse2(add(a[12:16], b[0:4]))
    lm, rm = a[4:8], b[8:12]
    wl, wr = mm(inv, a[8:12]), mm(inv, b[4:8])
    merged = (
        sub(a[0:4], mm(lm, wl)) + neg(mm(lm, wr)) + neg(mm(rm, wl)) + sub(b[12:16], mm(rm, wr))
    )
    return merged, wl + wr + inv + lm + rm


def merge_rhs(a, b, factors):
    inv, lm, rm = factors[8:12], factors[12:16], factors[16:20]
    w = mv(inv, add(a[2:4], b[0:2]))
    return sub(a[0:2], mv(lm, w)) + sub(b[2:4], mv(rm, w)), w


def tree_matrix(parts, stash):
    levels = []
    while len(parts) > 1:
        merged, kept = [], []
        for k in range(0, len(parts), 2):
            m, factors = merge_matrix(parts[k](), parts[k + 1]())
            merged.append(functools.partial(lambda v: v, m))
            kept.append(stash.put_all(factors))
        parts = merged
        levels.append(kept)
    return parts[0](), levels


def tree_rhs(parts, levels, stash):
    kept = []
    for level in levels:
        merged, saved = [], []
        for k, factors in enumerate(level):
            m, w = merge_rhs(parts[2 * k], parts[2 * k + 1], [None] * 8 + fetch(factors[8:20]))
            merged.append(m)
            saved.append(stash.put_all(w))
        parts = merged
        kept.append(saved)
    return parts[0], kept


def tree_back(joints, levels, results):
    spans = [joints]
    for level, saved in zip(reversed(levels), reversed(results)):
        finer = []
        for span, factors, w in zip(spans, level, saved):
            k = fetch(factors[:8])
            middle = sub(sub(fetch(w), mv(k[0:4], span[0:2])), mv(k[4:8], span[2:4]))
            finer.append(span[0:2] + middle)
            finer.append(middle + span[2:4])
        spans = finer
    return spans


def homes(lines, ring):
    return ring // 2, [spot % (ring // 2) for spot in (0, 1, -1, 2, -2)[: lines // 2]]


def ring_matrix(even, odd, stash):
    before = roll(odd, 1)
    d_even, l_even, u_even = add(even[0:4], before[12:16]), before[8:12], even[4:8]
    d_odd, l_odd, u_odd = add(odd[0:4], even[12:16]), even[8:12], odd[4:8]
    inv = inverse2(d_odd)
    alpha, beta = mm(l_even, roll(inv, 1)), mm(u_even, inv)
    low = neg(mm(alpha, roll(l_odd, 1)))
    high = neg(mm(beta, u_odd))
    mid = sub(sub(d_even, mm(alpha, roll(u_odd, 1))), mm(beta, l_odd))
    factors = [alpha + beta]
    half = d_even[0].shape[0]
    step = 1
    while step < half:
        inv_mid = inverse2(mid)
        alpha = mm(low, roll(inv_mid, step))
        beta = mm(high, roll(inv_mid, -step))
        low_b, low_a = roll(low, step), roll(low, -step)
        high_b, high_a = roll(high, step), roll(high, -step)
        mid = sub(sub(mid, mm(alpha, high_b)), mm(beta, low_a))
        low, high = neg(mm(alpha, low_b)), neg(mm(beta, high_a))
        factors.append(alpha + beta)
        step *= 2
    last = inverse2(add(add(low, mid), high))
    kept = [stash.put_all(level) for level in factors]
    return kept, stash.put_all(last), stash.put_all(mm(inv, l_odd) + mm(inv, u_odd) + inv)


def ring_rhs(even, odd, ring):
    kept, last, outer = ring
    before = roll(odd[2:4], 1)
    f_even, f_odd = add(even[0:2], before), add(odd[0:2], even[2:4])
    k = fetch(kept[0])
    f = sub(sub(f_even, mv(k[0:4], roll(f_odd, 1))), mv(k[4:8], f_odd))
    step = 1
    for level in kept[1:]:
        k = fetch(level)
        f = sub(sub(f, mv(k[0:4], roll(f, step))), mv(k[4:8], roll(f, -step)))
        step *= 2
    x_even = mv(fetch(last), f)
    after = roll(x_even, -1)
    k = fetch(outer)
    x_odd = sub(sub(mv(k[8:12], f_odd), mv(k[0:4], x_even)), mv(k[4:8], after))
    return x_even + x_odd, x_odd + after


def kernel(
    fields, ring_w, ring_n, rows_n,
    residual_hbm, cxi_hbm, ceta_hbm, dxi_hbm, deta_hbm, coupling_hbm,
    out_ref,
    residual, cxi, ceta, dxi, deta, coupling,
    turned_c, turned_r, turned_b, mixed, small_xi, small_eta,
    send_xi, recv_xi, back_send_xi, back_recv_xi,
    send_m, recv_m, send_r, recv_r, back_send_eta, back_recv_eta,
    joints_xi, joints_eta, stash_cells, stash_small, stash_ring,
    in_sems, send_xi_sem, recv_xi_sem, bsend_xi_sem, brecv_xi_sem,
    send_m_sem, recv_m_sem, send_r_sem, recv_r_sem, bsend_eta_sem, brecv_eta_sem,
):
    me_w, me_n = lax.axis_index("wrap"), lax.axis_index("normal")
    lines = 2 * fields
    cells_w, cells_n = LANES // SUBS, rows_n // SUBS
    small = Stash(stash_small)
    cell_store = Stash(stash_cells)

    pairs = [(cxi_hbm, cxi), (dxi_hbm, dxi), (residual_hbm, residual), (ceta_hbm, ceta), (deta_hbm, deta), (coupling_hbm, coupling)]
    loads = [pltpu.make_async_copy(s, t, in_sems.at[i]) for i, (s, t) in enumerate(pairs)]
    for load in loads:
        load.start()

    barrier = pltpu.get_barrier_semaphore()

    half, sites = homes(lines, ring_n)
    my_half = lax.div(me_n, half)
    my_spot = lax.rem(me_n, half)
    own_eta = functools.reduce(lambda a, b: a | b, [my_spot == spot for spot in sites])
    r_xi = lax.div(me_w * fields + ring_w - 1, ring_w)
    own_xi = lax.div(r_xi * ring_w, fields) == me_w

    def greet(axis, me, size):
        def one(o, carry):
            d = o + (o >= me).astype(jnp.int32)
            pl.semaphore_signal(barrier, inc=1, device_id={axis: d}, device_id_type=pl.DeviceIdType.MESH)
            return carry

        lax.fori_loop(0, size - 1, one, 0)

    @pl.when(own_eta)
    def _():
        greet("normal", me_n, ring_n)

    @pl.when(own_xi)
    def _():
        greet("wrap", me_w, ring_w)

    send_xi[...] = jnp.zeros_like(send_xi)
    back_send_xi[...] = jnp.zeros_like(back_send_xi)

    loads[0].wait()
    for f in range(fields):
        turned_c[pl.ds(f * LANES, LANES), :] = cxi[pl.ds(f * LANES, LANES), :].T
    loads[1].wait()
    turned_b[...] = dxi[...].T
    loads[2].wait()
    for f in range(fields):
        turned_r[pl.ds(f * LANES, LANES), :] = residual[pl.ds(f * LANES, LANES), :].T

    def every(ref, count, stride):
        return lambda j: ref[pl.ds(j, count, stride=stride), :]

    def tile(count):
        return lambda v: jnp.concatenate([v] * count, axis=0)

    rows_xi = fields * SUBS
    one_xi = jnp.float32(1.0)
    matrix, rhs, cells_xi = eliminate(
        cells_w, every(turned_c, rows_xi, cells_w), every(turned_b, SUBS, cells_w), tile(fields),
        every(turned_r, rows_xi, cells_w), one_xi, one_xi, cell_store, False,
    )
    for k, v in enumerate(matrix + rhs):
        small_xi[pl.ds(k * rows_xi, rows_xi), :] = v

    def packed(ref, rows, first, count):
        def part(g):
            return lambda: [ref[pl.ds(k * rows + first * SUBS + g, fields, stride=SUBS), :] for k in range(count)]

        return [part(g) for g in range(SUBS)]

    parts = packed(small_xi, rows_xi, 0, 16)
    whole, tree_xi = tree_matrix(parts, small)
    parts_r = [
        [small_xi[pl.ds(k * rows_xi + g, fields, stride=SUBS), :] for k in range(16, 20)] for g in range(SUBS)
    ]
    whole_r, tree_xi_r = tree_rhs(parts_r, tree_xi, small)
    for k, v in enumerate(whole + whole_r):
        send_xi[pl.ds(k, fields, stride=24), :] = v

    expected = fields - own_xi.astype(jnp.int32) + 2 * len(sites) - own_eta.astype(jnp.int32)
    pl.semaphore_wait(barrier, expected)

    def remote(src, dst, send_sem, recv_sem, axis, target):
        return pltpu.make_async_remote_copy(
            src_ref=src, dst_ref=dst, send_sem=send_sem, recv_sem=recv_sem,
            device_id={axis: target}, device_id_type=pl.DeviceIdType.MESH,
        )

    def to_owner(count, size, rows, src, dst, send_sem, recv_sem, axis, me):
        copies = []
        for r in range(count):
            owner = size * r // count
            copy = remote(
                src.at[pl.ds(r * rows, rows), :], dst.at[pl.ds(pl.multiple_of(me * rows, rows), rows), :],
                send_sem.at[r], recv_sem, axis, owner,
            )

            @pl.when(me != owner)
            def _():
                copy.start()

            @pl.when(me == owner)
            def _():
                dst[pl.ds(owner * rows, rows), :] = src[pl.ds(r * rows, rows), :]

            copies.append((owner, copy))
        return copies

    def await_rows(ref, rows, sem):
        slot = ref.at[pl.ds(0, rows), :]
        pltpu.make_async_copy(slot, slot, sem).wait()

    def hand_back(r, size, answer, src, dst, send_sem, recv_sem, axis, me):
        for k in range(4):
            src[pl.ds(k, size // 2, stride=16), :] = answer[0][k]
            src[pl.ds(8 + k, size // 2, stride=16), :] = answer[1][k]
        into = dst.at[pl.ds(pl.multiple_of(r * 8, 8), 8), :]

        def one(o, carry):
            d = o + (o >= me).astype(jnp.int32)
            remote(src.at[pl.ds(pl.multiple_of(d * 8, 8), 8), :], into, send_sem.at[d], recv_sem, axis, d).start()
            return carry

        lax.fori_loop(0, size - 1, one, 0)
        dst[pl.ds(pl.multiple_of(r * 8, 8), 8), :] = src[pl.ds(pl.multiple_of(me * 8, 8), 8), :]

    def wait_back(rows, owner, ref, sem):
        @pl.when(owner)
        def _():
            if rows > 8:
                await_rows(ref, rows - 8, sem)

        @pl.when(jnp.logical_not(owner))
        def _():
            await_rows(ref, rows, sem)

    def to_homes(rows, src, dst, send_sem, recv_sem):
        size = 2 * rows
        copies = []
        for side in range(2):
            for j, spot in enumerate(sites):
                target = side * half + spot
                begin = j * size
                copy = remote(
                    src.at[pl.ds(begin, size), :], dst.at[pl.ds(pl.multiple_of(me_n * size, size), size), :],
                    send_sem.at[side * len(sites) + j], recv_sem, "normal", target,
                )

                @pl.when(me_n != target)
                def _():
                    copy.start()

                @pl.when(me_n == target)
                def _():
                    dst[pl.ds(target * size, size), :] = src[pl.ds(begin, size), :]

                copies.append((target, copy))
        return copies

    def home_copy(j, d):
        return remote(
            back_send_eta.at[pl.ds(pl.multiple_of(d * 8, 8), 8), :],
            back_recv_eta.at[pl.ds(j * 8, 8), :],
            bsend_eta_sem.at[lax.rem(d, half)], brecv_eta_sem, "normal", d,
        )

    xi_copies = to_owner(fields, ring_w, 24, send_xi, recv_xi, send_xi_sem, recv_xi_sem, "wrap", me_w)

    loads[3].wait()
    loads[4].wait()
    rows_eta = lines * SUBS
    place = lax.rem(lax.broadcasted_iota(jnp.int32, (rows_eta, LANES), 0), SUBS)
    keep_left = jnp.where((place == 0) & (me_n == 0), 0.0, 1.0).astype(jnp.float32)
    keep_right = jnp.where((place == SUBS - 1) & (me_n == ring_n - 1), 0.0, 1.0).astype(jnp.float32)
    matrix, _, cells_eta = eliminate(
        cells_n, every(ceta, rows_eta, cells_n), every(deta, 2 * SUBS, cells_n), tile(fields),
        None, keep_left, keep_right, cell_store, True,
    )
    for k, v in enumerate(matrix):
        small_eta[pl.ds(k * rows_eta, rows_eta), :] = v


    @pl.when(own_xi)
    def _():
        await_rows(recv_xi, (ring_w - 1) * 24, recv_xi_sem)
        even = [recv_xi[pl.ds(k, ring_w // 2, stride=48), :] for k in range(20)]
        odd = [recv_xi[pl.ds(24 + k, ring_w // 2, stride=48), :] for k in range(20)]
        ring = ring_matrix(even[:16], odd[:16], Stash(stash_ring))
        answer = ring_rhs(even[16:], odd[16:], ring)
        hand_back(r_xi, ring_w, answer, back_send_xi, back_recv_xi, bsend_xi_sem, brecv_xi_sem, "wrap", me_w)

    trees_eta = []
    for h in range(2):
        whole, tree = tree_matrix(packed(small_eta, rows_eta, h * fields, 16), small)
        for k, v in enumerate(whole):
            send_m[pl.ds(h * fields * 16 + k, fields, stride=16), :] = v
        trees_eta.append(tree)
    m_copies = to_homes(16, send_m, recv_m, send_m_sem, recv_m_sem)

    def all_sent(me, copies):
        for owner, copy in copies:

            @pl.when(me != owner)
            def _():
                copy.wait_send()

    def place_joints(spans, ref, rows, first):
        for g, span in enumerate(spans):
            for k in range(4):
                ref[pl.ds(k * rows + first * SUBS + g, fields, stride=SUBS), :] = span[k]

    all_sent(me_w, xi_copies)

    wait_back(fields * 8, own_xi, back_recv_xi, brecv_xi_sem)
    joints = [back_recv_xi[pl.ds(k, fields, stride=8), :] for k in range(4)]
    place_joints(tree_back(joints, tree_xi, tree_xi_r), joints_xi, rows_xi, 0)

    def write_xi(j, value):
        turned_r[pl.ds(j, rows_xi, stride=cells_w), :] = value

    back(
        cells_w, cells_xi, [s[4] for s in cells_xi],
        [joints_xi[pl.ds(k * rows_xi, rows_xi), :] for k in range(4)], write_xi,
    )
    for f in range(fields):
        turned_c[pl.ds(f * LANES, LANES), :] = turned_r[pl.ds(f * LANES, LANES), :].T

    loads[5].wait()

    def mix(q, carry):
        start = pl.multiple_of(q * 16, 16)
        xi = [turned_c[pl.ds(j * LANES + start, 16), :] for j in range(fields)]
        for k in range(fields):
            total = None
            for j in range(fields):
                term = coupling[pl.ds((k * fields + j) * LANES + start, 16), :].astype(jnp.float32) * xi[j]
                total = term if total is None else total + term
            mixed[pl.ds(k * LANES + start, 16), :] = total
        return carry

    lax.fori_loop(0, LANES // 16, mix, 0)

    rhs, cells_eta_r = forward_rhs(cells_n, every(mixed, rows_eta, cells_n), cells_eta, cell_store)
    for k, v in enumerate(rhs):
        small_eta[pl.ds(k * rows_eta, rows_eta), :] = v
    trees_eta_r = []
    for h in range(2):
        parts_r = [part() for part in packed(small_eta, rows_eta, h * fields, 4)]
        whole_r, kept = tree_rhs(parts_r, trees_eta[h], small)
        for k, v in enumerate(whole_r):
            send_r[pl.ds(h * fields * 4 + k, fields, stride=4), :] = v
        trees_eta_r.append(kept)
    r_copies = to_homes(4, send_r, recv_r, send_r_sem, recv_r_sem)
    all_sent(me_n, m_copies)


    def each_home(act):
        for j, spot in enumerate(sites):

            @pl.when(my_spot == spot)
            def _():
                def one(o, carry):
                    act(home_copy(j, my_half * half + o + (o >= spot).astype(jnp.int32)))
                    return carry

                lax.fori_loop(0, half - 1, one, 0)

    @pl.when(own_eta)
    def _():
        await_rows(recv_m, (ring_n - 1) * 32, recv_m_sem)
        kept = Stash(stash_ring)

        def by_parity(ref, i, rows, count):
            slot = 2 * rows
            return [
                [ref[pl.ds(odd * slot + i * rows + k, ring_n // 2, stride=2 * slot), :] for k in range(count)]
                for odd in range(2)
            ]

        rings = [ring_matrix(*by_parity(recv_m, i, 16, 16), kept) for i in range(2)]
        await_rows(recv_r, (ring_n - 1) * 8, recv_r_sem)
        answers = [ring_rhs(*by_parity(recv_r, i, 4, 4), rings[i]) for i in range(2)]
        for i, answer in enumerate(answers):
            for k in range(4):
                for odd in range(2):
                    back_send_eta[pl.ds(odd * 8 + i * 4 + k, ring_n // 2, stride=16), :] = answer[odd][k]
        each_home(lambda copy: copy.start())
        for j, spot in enumerate(sites):

            @pl.when(my_spot == spot)
            def _():
                back_recv_eta[pl.ds(j * 8, 8), :] = back_send_eta[pl.ds(pl.multiple_of(me_n * 8, 8), 8), :]

    all_sent(me_n, r_copies)
    wait_back(lines * 4, own_eta, back_recv_eta, brecv_eta_sem)
    for h in range(2):
        joints = [back_recv_eta[pl.ds(h * fields * 4 + k, fields, stride=4), :] for k in range(4)]
        place_joints(tree_back(joints, trees_eta[h], trees_eta_r[h]), joints_eta, rows_eta, h * fields)

    def write_eta(j, value):
        out_ref[pl.ds(j, rows_eta, stride=cells_n), :] = value

    back(
        cells_n, cells_eta, cells_eta_r,
        [joints_eta[pl.ds(k * rows_eta, rows_eta), :] for k in range(4)], write_eta,
    )

    def drain(size, src, send_sem, axis, me):
        def one(o, carry):
            d = o + (o >= me).astype(jnp.int32)
            slot = src.at[pl.ds(pl.multiple_of(d * 8, 8), 8), :]
            remote(slot, slot, send_sem.at[d], send_sem.at[d], axis, d).wait_send()
            return carry

        lax.fori_loop(0, size - 1, one, 0)

    @pl.when(own_xi)
    def _():
        drain(ring_w, back_send_xi, bsend_xi_sem, "wrap", me_w)

    @pl.when(own_eta)
    def _():
        each_home(lambda copy: copy.wait_send())


def solution(mesh):
    ring_w, ring_n = mesh.shape["wrap"], mesh.shape["normal"]

    def local(residual, courant_xi, courant_eta, dissip_xi, dissip_eta, coupling):
        fields, _, rows_n, _ = residual.shape
        lines = 2 * fields
        flat = fields * LANES
        cells_w, cells_n = LANES // SUBS, rows_n // SUBS
        xi_rows, eta_rows = fields * SUBS, lines * SUBS
        pad = -(-fields // 8) * 8
        _, sites = homes(lines, ring_n)
        vmem = lambda rows, dtype=jnp.float32: pltpu.VMEM((rows, LANES), dtype)
        dma = lambda count: pltpu.SemaphoreType.DMA((count,))
        scratch = [
            vmem(flat), vmem(flat), vmem(flat), vmem(LANES), vmem(LANES), vmem(fields * flat, jnp.bfloat16),
            vmem(flat), vmem(flat), vmem(LANES), vmem(flat), vmem(20 * xi_rows), vmem(16 * eta_rows),
            vmem(fields * 24), vmem(ring_w * 24), vmem(ring_w * 8), vmem(fields * 8),
            vmem(lines * 16), vmem(ring_n * 32), vmem(lines * 4), vmem(ring_n * 8), vmem(ring_n * 8), vmem(lines * 4),
            vmem(4 * xi_rows), vmem(4 * eta_rows),
            vmem((cells_w - 2) * 5 * xi_rows + (cells_n - 2) * 10 * eta_rows),
            vmem((SUBS - 1) * 22 * 3 * pad),
            vmem(2 * (8 * 8 + 4 + 12) * max(8, ring_w // 2, ring_n // 2)),
            dma(6), dma(fields), pltpu.SemaphoreType.DMA, dma(ring_w), pltpu.SemaphoreType.DMA,
            dma(2 * len(sites)), pltpu.SemaphoreType.DMA, dma(2 * len(sites)), pltpu.SemaphoreType.DMA,
            dma(ring_n // 2), pltpu.SemaphoreType.DMA,
        ]
        out = pl.pallas_call(
            functools.partial(kernel, fields, ring_w, ring_n, rows_n),
            out_shape=jax.ShapeDtypeStruct((flat, LANES), jnp.float32),
            in_specs=[pl.BlockSpec(memory_space=pltpu.HBM)] * 6,
            out_specs=pl.BlockSpec(memory_space=pltpu.VMEM),
            scratch_shapes=scratch,
            compiler_params=pltpu.CompilerParams(
                collective_id=0, has_side_effects=True, vmem_limit_bytes=32 * 1024 * 1024
            ),
        )(
            *[pltpu.with_memory_space_constraint(v, pltpu.HBM) for v in (
            residual.reshape(flat, LANES), courant_xi.reshape(flat, LANES), courant_eta.reshape(flat, LANES),
            dissip_xi.reshape(LANES, LANES), dissip_eta.reshape(LANES, LANES), coupling.reshape(fields * flat, LANES),
            )]
        )
        return out.reshape(residual.shape)

    placed = (
        P(None, None, "normal", "wrap"),
        P(None, None, "normal", "wrap"),
        P(None, None, "normal", "wrap"),
        P(None, "normal", "wrap"),
        P(None, "normal", "wrap"),
        P(None, None, None, "normal", "wrap"),
    )
    return jax.shard_map(
        local, mesh=mesh, in_specs=placed, out_specs=P(None, None, "normal", "wrap"), check_vma=False
    )
```

```python
import functools

import jax
import jax.numpy as jnp
from jax import lax
from jax.experimental import pallas as pl
from jax.experimental.pallas import tpu as pltpu
from jax.sharding import PartitionSpec as P

LANES = 128
SUBS = 8


class Stash:
    def __init__(self, ref):
        self.ref, self.used = ref, 0

    def put(self, value):
        rows = value.shape[0]
        start = self.used
        self.used += -(-rows // 8) * 8
        assert self.used <= self.ref.shape[0]
        self.ref[pl.ds(start, rows), :] = value
        return lambda: self.ref[pl.ds(start, rows), :]

    def put_all(self, values):
        return [self.put(value) for value in values]


def fetch(handles):
    return [handle() for handle in handles]


def inverse2(m):
    scale = 1.0 / (m[0] * m[3] - m[1] * m[2])
    return [m[3] * scale, -(m[1] * scale), -(m[2] * scale), m[0] * scale]


def mm(a, b):
    return [
        a[0] * b[0] + a[1] * b[2],
        a[0] * b[1] + a[1] * b[3],
        a[2] * b[0] + a[3] * b[2],
        a[2] * b[1] + a[3] * b[3],
    ]


def mv(a, x):
    return [a[0] * x[0] + a[1] * x[1], a[2] * x[0] + a[3] * x[1]]


def sub(a, b):
    return [p - q for p, q in zip(a, b)]


def add(a, b):
    return [p + q for p, q in zip(a, b)]


def neg(a):
    return [-p for p in a]


def roll(values, shift):
    return [pltpu.roll(v, shift % v.shape[0], 0) for v in values]


def eliminate(cells, speed, damp, spread, source, keep_left, keep_right, stash, keep_rhs_factors):
    b = [damp(j) for j in range(cells)]
    c = [speed(j) for j in range(cells)]
    wide = [spread(v) for v in b]
    off = [spread(-2.0 * (b[j] + b[j + 1])) for j in range(cells - 1)]
    diag = [None] + [spread(1.0 + b[j - 1] + 4.0 * b[j] + b[j + 1]) for j in range(1, cells - 1)]
    diag.append(spread(1.0 + b[cells - 2] + 4.0 * b[cells - 1]))
    edge_l = wide[0] * keep_left
    edge_r = wide[-1] * keep_right
    diag.append(edge_r)
    skew = [0.25 * (c[j] + c[j + 1]) for j in range(cells - 1)]
    above = [off[j] + skew[j] for j in range(cells - 1)]
    below = [off[j] - skew[j] for j in range(cells - 1)]
    skew_l = 0.25 * c[0] * keep_left
    skew_r = 0.25 * c[-1] * keep_right
    above.append(-2.0 * edge_r + skew_r)
    below.append(-2.0 * edge_r - skew_r)
    ll = [edge_l, -2.0 * edge_l + skew_l, -2.0 * edge_l - skew_l, spread(1.0 + 4.0 * b[0] + b[1])]
    e, e_next = [edge_l, below[0]], [None, wide[1]]
    f, f_next = [edge_l, above[0]], [None, wide[1]]
    d, p, q, d_next = diag[1], above[1], below[1], diag[2]
    with_rhs = source is not None
    if with_rhs:
        r = [source(j) for j in range(cells)]
        r_left = [None, r[0]]
        here, after = r[1], r[2]
    saved = []
    for i in range(1, cells - 1):
        t = wide[i + 1] if i < cells - 2 else edge_r
        inv = 1.0 / d
        w1, w2 = inv * p, inv * t
        wl = [inv * e[0], inv * e[1]]
        keep = [w1, w2, wl[0], wl[1]]
        if with_rhs:
            wr = inv * here
            r_left = [-(f[0] * wr) if r_left[0] is None else r_left[0] - f[0] * wr, r_left[1] - f[1] * wr]
            tail = t * wr
            here, after = after - q * wr, (r[i + 2] - tail if i + 2 < cells else -tail)
            keep.append(wr)
        if keep_rhs_factors:
            keep += [inv, q, t, f[0], f[1]]
        saved.append(stash.put_all(keep))
        ll = [ll[0] - f[0] * wl[0], ll[1] - f[0] * wl[1], ll[2] - f[1] * wl[0], ll[3] - f[1] * wl[1]]
        e, e_next = (
            [-(q * wl[a]) if e_next[a] is None else e_next[a] - q * wl[a] for a in (0, 1)],
            [-(t * wl[a]) for a in (0, 1)],
        )
        f, f_next = (
            [-(f[a] * w1) if f_next[a] is None else f_next[a] - f[a] * w1 for a in (0, 1)],
            [-(f[a] * w2) for a in (0, 1)],
        )
        d, p, q, d_next = (
            d_next - q * w1,
            above[i + 1] - q * w2,
            below[i + 1] - t * w1,
            diag[i + 2] - t * w2,
        )
    matrix = ll + [f[0], f_next[0], f[1], f_next[1]] + [e[0], e[1], e_next[0], e_next[1]] + [d, p, q, d_next]
    rhs = r_left + [here, after] if with_rhs else None
    return matrix, rhs, saved


def forward_rhs(cells, source, saved, stash):
    r = [source(j) for j in range(cells)]
    r_left = [None, r[0]]
    here, after = r[1], r[2]
    kept = []
    for i in range(1, cells - 1):
        inv, q, t, f0, f1 = fetch(saved[i - 1][4:9])
        wr = inv * here
        kept.append(stash.put(wr))
        r_left = [-(f0 * wr) if r_left[0] is None else r_left[0] - f0 * wr, r_left[1] - f1 * wr]
        tail = t * wr
        here, after = after - q * wr, (r[i + 2] - tail if i + 2 < cells else -tail)
    return r_left + [here, after], kept


def back(cells, saved, results, joints, write):
    left, right = joints[:2], joints[2:]
    write(0, left[1])
    write(cells - 1, right[0])
    nearer, farther = right[0], right[1]
    for i in range(cells - 2, 0, -1):
        w1, w2, wl0, wl1 = fetch(saved[i - 1][:4])
        value = results[i - 1]() - wl0 * left[0] - wl1 * left[1] - w2 * farther - w1 * nearer
        write(i, value)
        nearer, farther = value, nearer


def merge_matrix(a, b):
    inv = inverse2(add(a[12:16], b[0:4]))
    lm, rm = a[4:8], b[8:12]
    wl, wr = mm(inv, a[8:12]), mm(inv, b[4:8])
    merged = (
        sub(a[0:4], mm(lm, wl)) + neg(mm(lm, wr)) + neg(mm(rm, wl)) + sub(b[12:16], mm(rm, wr))
    )
    return merged, wl + wr + inv + lm + rm


def merge_rhs(a, b, factors):
    inv, lm, rm = factors[8:12], factors[12:16], factors[16:20]
    w = mv(inv, add(a[2:4], b[0:2]))
    return sub(a[0:2], mv(lm, w)) + sub(b[2:4], mv(rm, w)), w


def tree_matrix(parts, stash):
    levels = []
    while len(parts) > 1:
        merged, kept = [], []
        for k in range(0, len(parts), 2):
            m, factors = merge_matrix(parts[k](), parts[k + 1]())
            merged.append(functools.partial(lambda v: v, m))
            kept.append(stash.put_all(factors))
        parts = merged
        levels.append(kept)
    return parts[0](), levels


def tree_rhs(parts, levels, stash):
    kept = []
    for level in levels:
        merged, saved = [], []
        for k, factors in enumerate(level):
            m, w = merge_rhs(parts[2 * k], parts[2 * k + 1], [None] * 8 + fetch(factors[8:20]))
            merged.append(m)
            saved.append(stash.put_all(w))
        parts = merged
        kept.append(saved)
    return parts[0], kept


def tree_back(joints, levels, results):
    spans = [joints]
    for level, saved in zip(reversed(levels), reversed(results)):
        finer = []
        for span, factors, w in zip(spans, level, saved):
            k = fetch(factors[:8])
            middle = sub(sub(fetch(w), mv(k[0:4], span[0:2])), mv(k[4:8], span[2:4]))
            finer.append(span[0:2] + middle)
            finer.append(middle + span[2:4])
        spans = finer
    return spans


def homes(lines, ring):
    return ring // 2, [spot % (ring // 2) for spot in (0, 1, -1, 2, -2)[: lines // 2]]


def ring_matrix(even, odd, stash):
    before = roll(odd, 1)
    d_even, l_even, u_even = add(even[0:4], before[12:16]), before[8:12], even[4:8]
    d_odd, l_odd, u_odd = add(odd[0:4], even[12:16]), even[8:12], odd[4:8]
    inv = inverse2(d_odd)
    alpha, beta = mm(l_even, roll(inv, 1)), mm(u_even, inv)
    low = neg(mm(alpha, roll(l_odd, 1)))
    high = neg(mm(beta, u_odd))
    mid = sub(sub(d_even, mm(alpha, roll(u_odd, 1))), mm(beta, l_odd))
    factors = [alpha + beta]
    half = d_even[0].shape[0]
    step = 1
    while step < half:
        inv_mid = inverse2(mid)
        alpha = mm(low, roll(inv_mid, step))
        beta = mm(high, roll(inv_mid, -step))
        low_b, low_a = roll(low, step), roll(low, -step)
        high_b, high_a = roll(high, step), roll(high, -step)
        mid = sub(sub(mid, mm(alpha, high_b)), mm(beta, low_a))
        low, high = neg(mm(alpha, low_b)), neg(mm(beta, high_a))
        factors.append(alpha + beta)
        step *= 2
    last = inverse2(add(add(low, mid), high))
    kept = [stash.put_all(level) for level in factors]
    return kept, stash.put_all(last), stash.put_all(mm(inv, l_odd) + mm(inv, u_odd) + inv)


def ring_rhs(even, odd, ring):
    kept, last, outer = ring
    before = roll(odd[2:4], 1)
    f_even, f_odd = add(even[0:2], before), add(odd[0:2], even[2:4])
    k = fetch(kept[0])
    f = sub(sub(f_even, mv(k[0:4], roll(f_odd, 1))), mv(k[4:8], f_odd))
    step = 1
    for level in kept[1:]:
        k = fetch(level)
        f = sub(sub(f, mv(k[0:4], roll(f, step))), mv(k[4:8], roll(f, -step)))
        step *= 2
    x_even = mv(fetch(last), f)
    after = roll(x_even, -1)
    k = fetch(outer)
    x_odd = sub(sub(mv(k[8:12], f_odd), mv(k[0:4], x_even)), mv(k[4:8], after))
    return x_even + x_odd, x_odd + after


def kernel(
    fields, ring_w, ring_n, rows_n,
    residual_hbm, cxi_hbm, ceta_hbm, dxi_hbm, deta_hbm, coupling_hbm,
    out_ref,
    residual, cxi, ceta, dxi, deta, coupling,
    turned_c, turned_r, turned_b, mixed, small_xi, small_eta,
    send_xi, recv_xi, back_send_xi, back_recv_xi,
    send_m, recv_m, send_r, recv_r, back_send_eta, back_recv_eta,
    joints_xi, joints_eta, stash_cells, stash_small, stash_ring,
    in_sems, send_xi_sem, recv_xi_sem, bsend_xi_sem, brecv_xi_sem,
    send_m_sem, recv_m_sem, send_r_sem, recv_r_sem, bsend_eta_sem, brecv_eta_sem,
):
    me_w, me_n = lax.axis_index("wrap"), lax.axis_index("normal")
    lines = 2 * fields
    cells_w, cells_n = LANES // SUBS, rows_n // SUBS
    small = Stash(stash_small)
    cell_store = Stash(stash_cells)

    pairs = [(cxi_hbm, cxi), (dxi_hbm, dxi), (residual_hbm, residual), (ceta_hbm, ceta), (deta_hbm, deta), (coupling_hbm, coupling)]
    loads = [pltpu.make_async_copy(s, t, in_sems.at[i]) for i, (s, t) in enumerate(pairs)]
    for load in loads[:3]:
        load.start()

    barrier = pltpu.get_barrier_semaphore()

    half, sites = homes(lines, ring_n)
    my_half = lax.div(me_n, half)
    my_spot = lax.rem(me_n, half)
    own_eta = functools.reduce(lambda a, b: a | b, [my_spot == spot for spot in sites])
    r_xi = lax.div(me_w * fields + ring_w - 1, ring_w)
    own_xi = lax.div(r_xi * ring_w, fields) == me_w

    def greet(axis, me, size):
        def one(o, carry):
            d = o + (o >= me).astype(jnp.int32)
            pl.semaphore_signal(barrier, inc=1, device_id={axis: d}, device_id_type=pl.DeviceIdType.MESH)
            return carry

        lax.fori_loop(0, size - 1, one, 0)

    @pl.when(own_eta)
    def _():
        greet("normal", me_n, ring_n)

    @pl.when(own_xi)
    def _():
        greet("wrap", me_w, ring_w)

    send_xi[...] = jnp.zeros_like(send_xi)
    back_send_xi[...] = jnp.zeros_like(back_send_xi)

    gap_w = cells_w + 1

    def spaced(ref, f, value):
        for g in range(SUBS):
            ref[pl.ds((f * SUBS + g) * gap_w, cells_w), :] = value[g * cells_w : (g + 1) * cells_w]

    loads[0].wait()
    for f in range(fields):
        spaced(turned_c, f, cxi[pl.ds(f * LANES, LANES), :].T)
    loads[1].wait()
    spaced(turned_b, 0, dxi[...].T)
    loads[2].wait()
    for load in loads[3:]:
        load.start()
    for f in range(fields):
        spaced(turned_r, f, residual[pl.ds(f * LANES, LANES), :].T)

    def every(ref, count, stride):
        return lambda j: ref[pl.ds(j, count, stride=stride), :]

    def tile(count):
        return lambda v: jnp.concatenate([v] * count, axis=0)

    gap = SUBS + 1

    def put_parts(ref, k, rows, value):
        for r in range(rows):
            ref[pl.ds((k * rows + r) * gap, SUBS), :] = value[r * SUBS : (r + 1) * SUBS]

    def get_parts(ref, k, rows):
        return jnp.concatenate([ref[pl.ds((k * rows + r) * gap, SUBS), :] for r in range(rows)], axis=0)

    rows_xi = fields * SUBS
    one_xi = jnp.float32(1.0)
    matrix, rhs, cells_xi = eliminate(
        cells_w, every(turned_c, rows_xi, gap_w), every(turned_b, SUBS, gap_w), tile(fields),
        every(turned_r, rows_xi, gap_w), one_xi, one_xi, cell_store, False,
    )
    for k, v in enumerate(matrix + rhs):
        put_parts(small_xi, k, fields, v)

    def packed(ref, rows, first, count):
        def part(g):
            return lambda: [ref[pl.ds((k * rows + first) * gap + g, fields, stride=gap), :] for k in range(count)]

        return [part(g) for g in range(SUBS)]

    parts = packed(small_xi, fields, 0, 16)
    whole, tree_xi = tree_matrix(parts, small)
    parts_r = [
        [small_xi[pl.ds(k * fields * gap + g, fields, stride=gap), :] for k in range(16, 20)] for g in range(SUBS)
    ]
    whole_r, tree_xi_r = tree_rhs(parts_r, tree_xi, small)
    for k, v in enumerate(whole + whole_r):
        send_xi[pl.ds(k, fields, stride=24), :] = v

    expected = fields - own_xi.astype(jnp.int32) + 2 * len(sites) - own_eta.astype(jnp.int32)
    pl.semaphore_wait(barrier, expected)

    def remote(src, dst, send_sem, recv_sem, axis, target):
        return pltpu.make_async_remote_copy(
            src_ref=src, dst_ref=dst, send_sem=send_sem, recv_sem=recv_sem,
            device_id={axis: target}, device_id_type=pl.DeviceIdType.MESH,
        )

    def to_owner(count, size, rows, src, dst, send_sem, recv_sem, axis, me):
        copies = []
        for r in range(count):
            owner = size * r // count
            copy = remote(
                src.at[pl.ds(r * rows, rows), :], dst.at[pl.ds(pl.multiple_of(me * rows, rows), rows), :],
                send_sem.at[r], recv_sem, axis, owner,
            )

            @pl.when(me != owner)
            def _():
                copy.start()

            @pl.when(me == owner)
            def _():
                dst[pl.ds(owner * rows, rows), :] = src[pl.ds(r * rows, rows), :]

            copies.append((owner, copy))
        return copies

    def await_rows(ref, rows, sem):
        slot = ref.at[pl.ds(0, rows), :]
        pltpu.make_async_copy(slot, slot, sem).wait()

    def hand_back(r, size, answer, src, dst, send_sem, recv_sem, axis, me):
        for k in range(4):
            src[pl.ds(k, size // 2, stride=16), :] = answer[0][k]
            src[pl.ds(8 + k, size // 2, stride=16), :] = answer[1][k]
        into = dst.at[pl.ds(pl.multiple_of(r * 8, 8), 8), :]

        def one(o, carry):
            d = o + (o >= me).astype(jnp.int32)
            remote(src.at[pl.ds(pl.multiple_of(d * 8, 8), 8), :], into, send_sem.at[d], recv_sem, axis, d).start()
            return carry

        lax.fori_loop(0, size - 1, one, 0)
        dst[pl.ds(pl.multiple_of(r * 8, 8), 8), :] = src[pl.ds(pl.multiple_of(me * 8, 8), 8), :]

    def wait_back(rows, owner, ref, sem):
        @pl.when(owner)
        def _():
            if rows > 8:
                await_rows(ref, rows - 8, sem)

        @pl.when(jnp.logical_not(owner))
        def _():
            await_rows(ref, rows, sem)

    def to_homes(rows, src, dst, send_sem, recv_sem):
        size = 2 * rows
        copies = []
        for turn in range(2):
            side = lax.rem(my_half + 1 + turn, 2)
            for j, spot in enumerate(sites):
                target = side * half + spot
                begin = j * size
                copy = remote(
                    src.at[pl.ds(begin, size), :], dst.at[pl.ds(pl.multiple_of(me_n * size, size), size), :],
                    send_sem.at[turn * len(sites) + j], recv_sem, "normal", target,
                )
                copies.append((target, copy))
                if turn == 0:
                    copy.start()
                    continue

                @pl.when(me_n != target)
                def _():
                    copy.start()

                @pl.when(me_n == target)
                def _():
                    dst[pl.ds(pl.multiple_of(me_n * size, size), size), :] = src[pl.ds(begin, size), :]

        return copies

    def home_copy(j, d):
        return remote(
            back_send_eta.at[pl.ds(pl.multiple_of(d * 8, 8), 8), :],
            back_recv_eta.at[pl.ds(j * 8, 8), :],
            bsend_eta_sem.at[lax.rem(d, half)], brecv_eta_sem, "normal", d,
        )

    xi_copies = to_owner(fields, ring_w, 24, send_xi, recv_xi, send_xi_sem, recv_xi_sem, "wrap", me_w)

    loads[3].wait()
    loads[4].wait()
    rows_eta = lines * SUBS
    place = lax.rem(lax.broadcasted_iota(jnp.int32, (rows_eta, LANES), 0), SUBS)
    keep_left = jnp.where((place == 0) & (me_n == 0), 0.0, 1.0).astype(jnp.float32)
    keep_right = jnp.where((place == SUBS - 1) & (me_n == ring_n - 1), 0.0, 1.0).astype(jnp.float32)
    matrix, _, cells_eta = eliminate(
        cells_n, every(ceta, rows_eta, cells_n), every(deta, 2 * SUBS, cells_n), tile(fields),
        None, keep_left, keep_right, cell_store, True,
    )
    for k, v in enumerate(matrix):
        put_parts(small_eta, k, lines, v)


    @pl.when(own_xi)
    def _():
        await_rows(recv_xi, (ring_w - 1) * 24, recv_xi_sem)
        even = [recv_xi[pl.ds(k, ring_w // 2, stride=48), :] for k in range(20)]
        odd = [recv_xi[pl.ds(24 + k, ring_w // 2, stride=48), :] for k in range(20)]
        ring = ring_matrix(even[:16], odd[:16], Stash(stash_ring))
        answer = ring_rhs(even[16:], odd[16:], ring)
        hand_back(r_xi, ring_w, answer, back_send_xi, back_recv_xi, bsend_xi_sem, brecv_xi_sem, "wrap", me_w)

    trees_eta = []
    for h in range(2):
        whole, tree = tree_matrix(packed(small_eta, lines, h * fields, 16), small)
        for k, v in enumerate(whole):
            send_m[pl.ds(h * fields * 16 + k, fields, stride=16), :] = v
        trees_eta.append(tree)
    m_copies = to_homes(16, send_m, recv_m, send_m_sem, recv_m_sem)

    def all_sent(me, copies):
        for owner, copy in copies:

            @pl.when(me != owner)
            def _():
                copy.wait_send()

    def place_joints(spans, ref, rows, first):
        for g, span in enumerate(spans):
            for k in range(4):
                ref[pl.ds((k * rows + first) * gap + g, fields, stride=gap), :] = span[k]

    all_sent(me_w, xi_copies)

    wait_back(fields * 8, own_xi, back_recv_xi, brecv_xi_sem)
    joints = [back_recv_xi[pl.ds(k, fields, stride=8), :] for k in range(4)]
    place_joints(tree_back(joints, tree_xi, tree_xi_r), joints_xi, fields, 0)

    def write_xi(j, value):
        turned_r[pl.ds(j, rows_xi, stride=gap_w), :] = value

    back(
        cells_w, cells_xi, [s[4] for s in cells_xi],
        [get_parts(joints_xi, k, fields) for k in range(4)], write_xi,
    )
    for f in range(fields):
        turned = [turned_r[pl.ds((f * SUBS + g) * gap_w, cells_w), :] for g in range(SUBS)]
        turned_c[pl.ds(f * LANES, LANES), :] = jnp.concatenate(turned, axis=0).T

    loads[5].wait()

    def mix(q, carry):
        start = pl.multiple_of(q * 16, 16)
        xi = [turned_c[pl.ds(j * LANES + start, 16), :] for j in range(fields)]
        for k in range(fields):
            total = None
            for j in range(fields):
                term = coupling[pl.ds((k * fields + j) * LANES + start, 16), :].astype(jnp.float32) * xi[j]
                total = term if total is None else total + term
            for half_rows in range(16 // cells_n):
                mixed[pl.ds((k * LANES // cells_n + q * (16 // cells_n) + half_rows) * (cells_n + 1), cells_n), :] = (
                    total[half_rows * cells_n : (half_rows + 1) * cells_n]
                )
        return carry

    lax.fori_loop(0, LANES // 16, mix, 0)

    rhs, cells_eta_r = forward_rhs(cells_n, every(mixed, rows_eta, cells_n + 1), cells_eta, cell_store)
    for k, v in enumerate(rhs):
        put_parts(small_eta, k, lines, v)
    trees_eta_r = []
    for h in range(2):
        parts_r = [part() for part in packed(small_eta, lines, h * fields, 4)]
        whole_r, kept = tree_rhs(parts_r, trees_eta[h], small)
        for k, v in enumerate(whole_r):
            send_r[pl.ds(h * fields * 4 + k, fields, stride=4), :] = v
        trees_eta_r.append(kept)
    r_copies = to_homes(4, send_r, recv_r, send_r_sem, recv_r_sem)
    all_sent(me_n, m_copies)


    def each_home(act):
        for j, spot in enumerate(sites):

            @pl.when(my_spot == spot)
            def _():
                def one(o, carry):
                    act(home_copy(j, my_half * half + o + (o >= spot).astype(jnp.int32)))
                    return carry

                lax.fori_loop(0, half - 1, one, 0)

    @pl.when(own_eta)
    def _():
        await_rows(recv_m, (ring_n - 1) * 32, recv_m_sem)
        kept = Stash(stash_ring)

        def by_parity(ref, i, rows, count):
            slot = 2 * rows
            return [
                [ref[pl.ds(odd * slot + i * rows + k, ring_n // 2, stride=2 * slot), :] for k in range(count)]
                for odd in range(2)
            ]

        rings = [ring_matrix(*by_parity(recv_m, i, 16, 16), kept) for i in range(2)]
        await_rows(recv_r, (ring_n - 1) * 8, recv_r_sem)
        answers = [ring_rhs(*by_parity(recv_r, i, 4, 4), rings[i]) for i in range(2)]
        for i, answer in enumerate(answers):
            for k in range(4):
                for odd in range(2):
                    back_send_eta[pl.ds(odd * 8 + i * 4 + k, ring_n // 2, stride=16), :] = answer[odd][k]
        each_home(lambda copy: copy.start())
        for j, spot in enumerate(sites):

            @pl.when(my_spot == spot)
            def _():
                back_recv_eta[pl.ds(j * 8, 8), :] = back_send_eta[pl.ds(pl.multiple_of(me_n * 8, 8), 8), :]

    all_sent(me_n, r_copies)
    wait_back(lines * 4, own_eta, back_recv_eta, brecv_eta_sem)
    for h in range(2):
        joints = [back_recv_eta[pl.ds(h * fields * 4 + k, fields, stride=4), :] for k in range(4)]
        place_joints(tree_back(joints, trees_eta[h], trees_eta_r[h]), joints_eta, lines, h * fields)

    def write_eta(j, value):
        out_ref[pl.ds(j, rows_eta, stride=cells_n), :] = value

    back(
        cells_n, cells_eta, cells_eta_r,
        [get_parts(joints_eta, k, lines) for k in range(4)], write_eta,
    )

    def drain(size, src, send_sem, axis, me):
        def one(o, carry):
            d = o + (o >= me).astype(jnp.int32)
            slot = src.at[pl.ds(pl.multiple_of(d * 8, 8), 8), :]
            remote(slot, slot, send_sem.at[d], send_sem.at[d], axis, d).wait_send()
            return carry

        lax.fori_loop(0, size - 1, one, 0)

    @pl.when(own_xi)
    def _():
        drain(ring_w, back_send_xi, bsend_xi_sem, "wrap", me_w)

    @pl.when(own_eta)
    def _():
        each_home(lambda copy: copy.wait_send())


def solution(mesh):
    ring_w, ring_n = mesh.shape["wrap"], mesh.shape["normal"]

    def local(residual, courant_xi, courant_eta, dissip_xi, dissip_eta, coupling):
        fields, _, rows_n, _ = residual.shape
        lines = 2 * fields
        flat = fields * LANES
        cells_w, cells_n = LANES // SUBS, rows_n // SUBS
        xi_rows, eta_rows = fields * SUBS, lines * SUBS
        pad = -(-fields // 8) * 8
        _, sites = homes(lines, ring_n)
        vmem = lambda rows, dtype=jnp.float32: pltpu.VMEM((rows, LANES), dtype)
        dma = lambda count: pltpu.SemaphoreType.DMA((count,))
        scratch = [
            vmem(flat), vmem(flat), vmem(flat), vmem(LANES), vmem(LANES), vmem(fields * flat, jnp.bfloat16),
            vmem(flat + xi_rows), vmem(flat + xi_rows), vmem(LANES + SUBS), vmem(flat + eta_rows), vmem(20 * fields * (SUBS + 1)), vmem(16 * lines * (SUBS + 1)),
            vmem(fields * 24), vmem(ring_w * 24), vmem(ring_w * 8), vmem(fields * 8),
            vmem(lines * 16), vmem(ring_n * 32), vmem(lines * 4), vmem(ring_n * 8), vmem(ring_n * 8), vmem(lines * 4),
            vmem(4 * fields * (SUBS + 1)), vmem(4 * lines * (SUBS + 1)),
            vmem((cells_w - 2) * 5 * xi_rows + (cells_n - 2) * 10 * eta_rows),
            vmem((SUBS - 1) * 22 * 3 * pad),
            vmem(2 * (8 * 8 + 4 + 12) * max(8, ring_w // 2, ring_n // 2)),
            dma(6), dma(fields), pltpu.SemaphoreType.DMA, dma(ring_w), pltpu.SemaphoreType.DMA,
            dma(2 * len(sites)), pltpu.SemaphoreType.DMA, dma(2 * len(sites)), pltpu.SemaphoreType.DMA,
            dma(ring_n // 2), pltpu.SemaphoreType.DMA,
        ]
        out = pl.pallas_call(
            functools.partial(kernel, fields, ring_w, ring_n, rows_n),
            out_shape=jax.ShapeDtypeStruct((flat, LANES), jnp.float32),
            in_specs=[pl.BlockSpec(memory_space=pltpu.HBM)] * 6,
            out_specs=pl.BlockSpec(memory_space=pltpu.VMEM),
            scratch_shapes=scratch,
            compiler_params=pltpu.CompilerParams(
                collective_id=0, has_side_effects=True, vmem_limit_bytes=32 * 1024 * 1024
            ),
        )(
            *[pltpu.with_memory_space_constraint(v, pltpu.HBM) for v in (
            residual.reshape(flat, LANES), courant_xi.reshape(flat, LANES), courant_eta.reshape(flat, LANES),
            dissip_xi.reshape(LANES, LANES), dissip_eta.reshape(LANES, LANES), coupling.reshape(fields * flat, LANES),
            )]
        )
        return out.reshape(residual.shape)

    placed = (
        P(None, None, "normal", "wrap"),
        P(None, None, "normal", "wrap"),
        P(None, None, "normal", "wrap"),
        P(None, "normal", "wrap"),
        P(None, "normal", "wrap"),
        P(None, None, None, "normal", "wrap"),
    )
    return jax.shard_map(
        local, mesh=mesh, in_specs=placed, out_specs=P(None, None, "normal", "wrap"), check_vma=False
    )
```

```python
import functools

import jax
import jax.numpy as jnp
from jax import lax
from jax.experimental import pallas as pl
from jax.experimental.pallas import tpu as pltpu
from jax.sharding import PartitionSpec as P

LANES = 128
SUBS = 8


class Stash:
    def __init__(self, ref):
        self.ref, self.used = ref, 0

    def put(self, value):
        rows = value.shape[0]
        start = self.used
        self.used += -(-rows // 8) * 8
        assert self.used <= self.ref.shape[0]
        self.ref[pl.ds(start, rows), :] = value
        return lambda: self.ref[pl.ds(start, rows), :]

    def put_all(self, values):
        return [self.put(value) for value in values]


def fetch(handles):
    return [handle() for handle in handles]


def inverse2(m):
    scale = 1.0 / (m[0] * m[3] - m[1] * m[2])
    return [m[3] * scale, -(m[1] * scale), -(m[2] * scale), m[0] * scale]


def mm(a, b):
    return [
        a[0] * b[0] + a[1] * b[2],
        a[0] * b[1] + a[1] * b[3],
        a[2] * b[0] + a[3] * b[2],
        a[2] * b[1] + a[3] * b[3],
    ]


def mv(a, x):
    return [a[0] * x[0] + a[1] * x[1], a[2] * x[0] + a[3] * x[1]]


def sub(a, b):
    return [p - q for p, q in zip(a, b)]


def add(a, b):
    return [p + q for p, q in zip(a, b)]


def neg(a):
    return [-p for p in a]


def roll(values, shift):
    return [pltpu.roll(v, shift % v.shape[0], 0) for v in values]


def eliminate(cells, speed, damp, spread, source, keep_left, keep_right, stash, keep_rhs_factors):
    b = [damp(j) for j in range(cells)]
    c = [speed(j) for j in range(cells)]
    wide = [spread(v) for v in b]
    off = [spread(-2.0 * (b[j] + b[j + 1])) for j in range(cells - 1)]
    diag = [None] + [spread(1.0 + b[j - 1] + 4.0 * b[j] + b[j + 1]) for j in range(1, cells - 1)]
    diag.append(spread(1.0 + b[cells - 2] + 4.0 * b[cells - 1]))
    edge_l = wide[0] * keep_left
    edge_r = wide[-1] * keep_right
    diag.append(edge_r)
    skew = [0.25 * (c[j] + c[j + 1]) for j in range(cells - 1)]
    above = [off[j] + skew[j] for j in range(cells - 1)]
    below = [off[j] - skew[j] for j in range(cells - 1)]
    skew_l = 0.25 * c[0] * keep_left
    skew_r = 0.25 * c[-1] * keep_right
    above.append(-2.0 * edge_r + skew_r)
    below.append(-2.0 * edge_r - skew_r)
    ll = [edge_l, -2.0 * edge_l + skew_l, -2.0 * edge_l - skew_l, spread(1.0 + 4.0 * b[0] + b[1])]
    e, e_next = [edge_l, below[0]], [None, wide[1]]
    f, f_next = [edge_l, above[0]], [None, wide[1]]
    d, p, q, d_next = diag[1], above[1], below[1], diag[2]
    with_rhs = source is not None
    if with_rhs:
        r = [source(j) for j in range(cells)]
        r_left = [None, r[0]]
        here, after = r[1], r[2]
    saved = []
    for i in range(1, cells - 1):
        t = wide[i + 1] if i < cells - 2 else edge_r
        inv = 1.0 / d
        w1, w2 = inv * p, inv * t
        wl = [inv * e[0], inv * e[1]]
        keep = [w1, w2, wl[0], wl[1]]
        if with_rhs:
            wr = inv * here
            r_left = [-(f[0] * wr) if r_left[0] is None else r_left[0] - f[0] * wr, r_left[1] - f[1] * wr]
            tail = t * wr
            here, after = after - q * wr, (r[i + 2] - tail if i + 2 < cells else -tail)
            keep.append(wr)
        if keep_rhs_factors:
            keep += [inv, q, t, f[0], f[1]]
        saved.append(stash.put_all(keep))
        ll = [ll[0] - f[0] * wl[0], ll[1] - f[0] * wl[1], ll[2] - f[1] * wl[0], ll[3] - f[1] * wl[1]]
        e, e_next = (
            [-(q * wl[a]) if e_next[a] is None else e_next[a] - q * wl[a] for a in (0, 1)],
            [-(t * wl[a]) for a in (0, 1)],
        )
        f, f_next = (
            [-(f[a] * w1) if f_next[a] is None else f_next[a] - f[a] * w1 for a in (0, 1)],
            [-(f[a] * w2) for a in (0, 1)],
        )
        d, p, q, d_next = (
            d_next - q * w1,
            above[i + 1] - q * w2,
            below[i + 1] - t * w1,
            diag[i + 2] - t * w2,
        )
    matrix = ll + [f[0], f_next[0], f[1], f_next[1]] + [e[0], e[1], e_next[0], e_next[1]] + [d, p, q, d_next]
    rhs = r_left + [here, after] if with_rhs else None
    return matrix, rhs, saved


def forward_rhs(cells, source, saved, stash):
    r = [source(j) for j in range(cells)]
    r_left = [None, r[0]]
    here, after = r[1], r[2]
    kept = []
    for i in range(1, cells - 1):
        inv, q, t, f0, f1 = fetch(saved[i - 1][4:9])
        wr = inv * here
        kept.append(stash.put(wr))
        r_left = [-(f0 * wr) if r_left[0] is None else r_left[0] - f0 * wr, r_left[1] - f1 * wr]
        tail = t * wr
        here, after = after - q * wr, (r[i + 2] - tail if i + 2 < cells else -tail)
    return r_left + [here, after], kept


def back(cells, saved, results, joints, write):
    left, right = joints[:2], joints[2:]
    write(0, left[1])
    write(cells - 1, right[0])
    nearer, farther = right[0], right[1]
    for i in range(cells - 2, 0, -1):
        w1, w2, wl0, wl1 = fetch(saved[i - 1][:4])
        value = results[i - 1]() - wl0 * left[0] - wl1 * left[1] - w2 * farther - w1 * nearer
        write(i, value)
        nearer, farther = value, nearer


def merge_matrix(a, b):
    inv = inverse2(add(a[12:16], b[0:4]))
    lm, rm = a[4:8], b[8:12]
    wl, wr = mm(inv, a[8:12]), mm(inv, b[4:8])
    merged = (
        sub(a[0:4], mm(lm, wl)) + neg(mm(lm, wr)) + neg(mm(rm, wl)) + sub(b[12:16], mm(rm, wr))
    )
    return merged, wl + wr + inv + lm + rm


def merge_rhs(a, b, factors):
    inv, lm, rm = factors[8:12], factors[12:16], factors[16:20]
    w = mv(inv, add(a[2:4], b[0:2]))
    return sub(a[0:2], mv(lm, w)) + sub(b[2:4], mv(rm, w)), w


def tree_matrix(parts, stash):
    levels = []
    while len(parts) > 1:
        merged, kept = [], []
        for k in range(0, len(parts), 2):
            m, factors = merge_matrix(parts[k](), parts[k + 1]())
            merged.append(functools.partial(lambda v: v, m))
            kept.append(stash.put_all(factors))
        parts = merged
        levels.append(kept)
    return parts[0](), levels


def tree_rhs(parts, levels, stash):
    kept = []
    for level in levels:
        merged, saved = [], []
        for k, factors in enumerate(level):
            m, w = merge_rhs(parts[2 * k], parts[2 * k + 1], [None] * 8 + fetch(factors[8:20]))
            merged.append(m)
            saved.append(stash.put_all(w))
        parts = merged
        kept.append(saved)
    return parts[0], kept


def tree_back(joints, levels, results):
    spans = [joints]
    for level, saved in zip(reversed(levels), reversed(results)):
        finer = []
        for span, factors, w in zip(spans, level, saved):
            k = fetch(factors[:8])
            middle = sub(sub(fetch(w), mv(k[0:4], span[0:2])), mv(k[4:8], span[2:4]))
            finer.append(span[0:2] + middle)
            finer.append(middle + span[2:4])
        spans = finer
    return spans


def homes(lines, ring):
    return ring // 2, [spot % (ring // 2) for spot in (0, 1, -1, 2, -2)[: lines // 2]]


def ring_matrix(even, odd, stash):
    before = roll(odd, 1)
    d_even, l_even, u_even = add(even[0:4], before[12:16]), before[8:12], even[4:8]
    d_odd, l_odd, u_odd = add(odd[0:4], even[12:16]), even[8:12], odd[4:8]
    inv = inverse2(d_odd)
    alpha, beta = mm(l_even, roll(inv, 1)), mm(u_even, inv)
    low = neg(mm(alpha, roll(l_odd, 1)))
    high = neg(mm(beta, u_odd))
    mid = sub(sub(d_even, mm(alpha, roll(u_odd, 1))), mm(beta, l_odd))
    factors = [alpha + beta]
    half = d_even[0].shape[0]
    step = 1
    while step < half:
        inv_mid = inverse2(mid)
        alpha = mm(low, roll(inv_mid, step))
        beta = mm(high, roll(inv_mid, -step))
        low_b, low_a = roll(low, step), roll(low, -step)
        high_b, high_a = roll(high, step), roll(high, -step)
        mid = sub(sub(mid, mm(alpha, high_b)), mm(beta, low_a))
        low, high = neg(mm(alpha, low_b)), neg(mm(beta, high_a))
        factors.append(alpha + beta)
        step *= 2
    last = inverse2(add(add(low, mid), high))
    kept = [stash.put_all(level) for level in factors]
    return kept, stash.put_all(last), stash.put_all(mm(inv, l_odd) + mm(inv, u_odd) + inv)


def ring_rhs(even, odd, ring):
    kept, last, outer = ring
    before = roll(odd[2:4], 1)
    f_even, f_odd = add(even[0:2], before), add(odd[0:2], even[2:4])
    k = fetch(kept[0])
    f = sub(sub(f_even, mv(k[0:4], roll(f_odd, 1))), mv(k[4:8], f_odd))
    step = 1
    for level in kept[1:]:
        k = fetch(level)
        f = sub(sub(f, mv(k[0:4], roll(f, step))), mv(k[4:8], roll(f, -step)))
        step *= 2
    x_even = mv(fetch(last), f)
    after = roll(x_even, -1)
    k = fetch(outer)
    x_odd = sub(sub(mv(k[8:12], f_odd), mv(k[0:4], x_even)), mv(k[4:8], after))
    return x_even + x_odd, x_odd + after


def kernel(
    fields, ring_w, ring_n, rows_n,
    residual_hbm, cxi_hbm, ceta_hbm, dxi_hbm, deta_hbm, coupling_hbm,
    out_ref,
    residual, cxi, ceta, dxi, deta, coupling,
    turned_c, turned_r, turned_b, mixed, small_xi, small_eta,
    send_xi, recv_xi, back_send_xi, back_recv_xi,
    send_m, recv_m, send_r, recv_r, back_send_eta, back_recv_eta,
    joints_xi, joints_eta, stash_cells, stash_small, stash_ring,
    in_sems, send_xi_sem, recv_xi_sem, bsend_xi_sem, brecv_xi_sem,
    send_m_sem, recv_m_sem, send_r_sem, recv_r_sem, bsend_eta_sem, brecv_eta_sem,
):
    me_w, me_n = lax.axis_index("wrap"), lax.axis_index("normal")
    lines = 2 * fields
    cells_w, cells_n = LANES // SUBS, rows_n // SUBS
    small = Stash(stash_small)
    cell_store = Stash(stash_cells)

    pairs = [(cxi_hbm, cxi), (dxi_hbm, dxi), (residual_hbm, residual), (ceta_hbm, ceta), (deta_hbm, deta), (coupling_hbm, coupling)]
    loads = [pltpu.make_async_copy(s, t, in_sems.at[i]) for i, (s, t) in enumerate(pairs)]
    for load in loads[:3]:
        load.start()

    barrier = pltpu.get_barrier_semaphore()

    half, sites = homes(lines, ring_n)
    my_half = lax.div(me_n, half)
    my_spot = lax.rem(me_n, half)
    own_eta = functools.reduce(lambda a, b: a | b, [my_spot == spot for spot in sites])
    r_xi = lax.div(me_w * fields + ring_w - 1, ring_w)
    own_xi = lax.div(r_xi * ring_w, fields) == me_w

    def greet(axis, me, size):
        def one(o, carry):
            d = o + (o >= me).astype(jnp.int32)
            pl.semaphore_signal(barrier, inc=1, device_id={axis: d}, device_id_type=pl.DeviceIdType.MESH)
            return carry

        lax.fori_loop(0, size - 1, one, 0)

    @pl.when(own_eta)
    def _():
        greet("normal", me_n, ring_n)

    @pl.when(own_xi)
    def _():
        greet("wrap", me_w, ring_w)

    send_xi[...] = jnp.zeros_like(send_xi)
    back_send_xi[...] = jnp.zeros_like(back_send_xi)

    gap_w = cells_w + 1

    def spaced(ref, f, value):
        for g in range(SUBS):
            ref[pl.ds((f * SUBS + g) * gap_w, cells_w), :] = value[g * cells_w : (g + 1) * cells_w]

    loads[0].wait()
    for f in range(fields):
        spaced(turned_c, f, cxi[pl.ds(f * LANES, LANES), :].T)
    loads[1].wait()
    spaced(turned_b, 0, dxi[...].T)
    loads[2].wait()
    for load in loads[3:]:
        load.start()
    for f in range(fields):
        spaced(turned_r, f, residual[pl.ds(f * LANES, LANES), :].T)

    def every(ref, count, stride):
        return lambda j: ref[pl.ds(j, count, stride=stride), :]

    def tile(count):
        return lambda v: jnp.concatenate([v] * count, axis=0)

    gap = SUBS + 1

    def put_parts(ref, k, rows, value):
        for r in range(rows):
            ref[pl.ds((k * rows + r) * gap, SUBS), :] = value[r * SUBS : (r + 1) * SUBS]

    def get_parts(ref, k, rows):
        return jnp.concatenate([ref[pl.ds((k * rows + r) * gap, SUBS), :] for r in range(rows)], axis=0)

    rows_xi = fields * SUBS
    one_xi = jnp.float32(1.0)
    matrix, rhs, cells_xi = eliminate(
        cells_w, every(turned_c, rows_xi, gap_w), every(turned_b, SUBS, gap_w), tile(fields),
        every(turned_r, rows_xi, gap_w), one_xi, one_xi, cell_store, False,
    )
    for k, v in enumerate(matrix + rhs):
        put_parts(small_xi, k, fields, v)

    def packed(ref, rows, first, count):
        def part(g):
            return lambda: [ref[pl.ds((k * rows + first) * gap + g, fields, stride=gap), :] for k in range(count)]

        return [part(g) for g in range(SUBS)]

    parts = packed(small_xi, fields, 0, 16)
    whole, tree_xi = tree_matrix(parts, small)
    parts_r = [
        [small_xi[pl.ds(k * fields * gap + g, fields, stride=gap), :] for k in range(16, 20)] for g in range(SUBS)
    ]
    whole_r, tree_xi_r = tree_rhs(parts_r, tree_xi, small)
    for k, v in enumerate(whole + whole_r):
        send_xi[pl.ds(k, fields, stride=24), :] = v

    expected = fields - own_xi.astype(jnp.int32) + 2 * len(sites) - own_eta.astype(jnp.int32)
    pl.semaphore_wait(barrier, expected)

    def remote(src, dst, send_sem, recv_sem, axis, target):
        return pltpu.make_async_remote_copy(
            src_ref=src, dst_ref=dst, send_sem=send_sem, recv_sem=recv_sem,
            device_id={axis: target}, device_id_type=pl.DeviceIdType.MESH,
        )

    def to_owner(count, size, rows, src, dst, send_sem, recv_sem, axis, me):
        copies = []
        for r in range(count):
            owner = size * r // count
            copy = remote(
                src.at[pl.ds(r * rows, rows), :], dst.at[pl.ds(pl.multiple_of(me * rows, rows), rows), :],
                send_sem.at[r], recv_sem, axis, owner,
            )

            @pl.when(me != owner)
            def _():
                copy.start()

            @pl.when(me == owner)
            def _():
                dst[pl.ds(owner * rows, rows), :] = src[pl.ds(r * rows, rows), :]

            copies.append((owner, copy))
        return copies

    def await_rows(ref, rows, sem):
        slot = ref.at[pl.ds(0, rows), :]
        pltpu.make_async_copy(slot, slot, sem).wait()

    def hand_back(r, size, answer, src, dst, send_sem, recv_sem, axis, me):
        for k in range(4):
            src[pl.ds(k, size // 2, stride=16), :] = answer[0][k]
            src[pl.ds(8 + k, size // 2, stride=16), :] = answer[1][k]
        into = dst.at[pl.ds(pl.multiple_of(r * 8, 8), 8), :]

        def one(o, carry):
            d = o + (o >= me).astype(jnp.int32)
            remote(src.at[pl.ds(pl.multiple_of(d * 8, 8), 8), :], into, send_sem.at[d], recv_sem, axis, d).start()
            return carry

        lax.fori_loop(0, size - 1, one, 0)
        dst[pl.ds(pl.multiple_of(r * 8, 8), 8), :] = src[pl.ds(pl.multiple_of(me * 8, 8), 8), :]

    def wait_back(rows, owner, ref, sem):
        @pl.when(owner)
        def _():
            if rows > 8:
                await_rows(ref, rows - 8, sem)

        @pl.when(jnp.logical_not(owner))
        def _():
            await_rows(ref, rows, sem)

    def to_homes(rows, src, dst, send_sem, recv_sem):
        size = 2 * rows
        copies = []
        for turn in range(2):
            side = lax.rem(my_half + 1 + turn, 2)
            for j, spot in enumerate(sites):
                target = side * half + spot
                begin = j * size
                copy = remote(
                    src.at[pl.ds(begin, size), :], dst.at[pl.ds(pl.multiple_of(me_n * size, size), size), :],
                    send_sem.at[turn * len(sites) + j], recv_sem, "normal", target,
                )
                copies.append((target, copy))
                if turn == 0:
                    copy.start()
                    continue

                @pl.when(me_n != target)
                def _():
                    copy.start()

                @pl.when(me_n == target)
                def _():
                    dst[pl.ds(pl.multiple_of(me_n * size, size), size), :] = src[pl.ds(begin, size), :]

        return copies

    def home_copy(j, d):
        return remote(
            back_send_eta.at[pl.ds(pl.multiple_of(d * 8, 8), 8), :],
            back_recv_eta.at[pl.ds(j * 8, 8), :],
            bsend_eta_sem.at[lax.rem(d, half)], brecv_eta_sem, "normal", d,
        )

    xi_copies = to_owner(fields, ring_w, 24, send_xi, recv_xi, send_xi_sem, recv_xi_sem, "wrap", me_w)

    loads[3].wait()
    loads[4].wait()
    rows_eta = lines * SUBS
    place = lax.rem(lax.broadcasted_iota(jnp.int32, (rows_eta, LANES), 0), SUBS)
    keep_left = jnp.where((place == 0) & (me_n == 0), 0.0, 1.0).astype(jnp.float32)
    keep_right = jnp.where((place == SUBS - 1) & (me_n == ring_n - 1), 0.0, 1.0).astype(jnp.float32)
    matrix, _, cells_eta = eliminate(
        cells_n, every(ceta, rows_eta, cells_n), every(deta, 2 * SUBS, cells_n), tile(fields),
        None, keep_left, keep_right, cell_store, True,
    )
    for k, v in enumerate(matrix):
        put_parts(small_eta, k, lines, v)


    @pl.when(own_xi)
    def _():
        await_rows(recv_xi, (ring_w - 1) * 24, recv_xi_sem)
        even = [recv_xi[pl.ds(k, ring_w // 2, stride=48), :] for k in range(20)]
        odd = [recv_xi[pl.ds(24 + k, ring_w // 2, stride=48), :] for k in range(20)]
        ring = ring_matrix(even[:16], odd[:16], Stash(stash_ring))
        answer = ring_rhs(even[16:], odd[16:], ring)
        hand_back(r_xi, ring_w, answer, back_send_xi, back_recv_xi, bsend_xi_sem, brecv_xi_sem, "wrap", me_w)

    trees_eta = []
    for h in range(2):
        whole, tree = tree_matrix(packed(small_eta, lines, h * fields, 16), small)
        for k, v in enumerate(whole):
            send_m[pl.ds(h * fields * 16 + k, fields, stride=16), :] = v
        trees_eta.append(tree)
    m_copies = to_homes(16, send_m, recv_m, send_m_sem, recv_m_sem)

    def all_sent(me, copies):
        for owner, copy in copies:

            @pl.when(me != owner)
            def _():
                copy.wait_send()

    def place_joints(spans, ref, rows, first):
        for g, span in enumerate(spans):
            for k in range(4):
                ref[pl.ds((k * rows + first) * gap + g, fields, stride=gap), :] = span[k]

    all_sent(me_w, xi_copies)

    wait_back(fields * 8, own_xi, back_recv_xi, brecv_xi_sem)
    joints = [back_recv_xi[pl.ds(k, fields, stride=8), :] for k in range(4)]
    place_joints(tree_back(joints, tree_xi, tree_xi_r), joints_xi, fields, 0)

    def write_xi(j, value):
        turned_r[pl.ds(j, rows_xi, stride=gap_w), :] = value

    back(
        cells_w, cells_xi, [s[4] for s in cells_xi],
        [get_parts(joints_xi, k, fields) for k in range(4)], write_xi,
    )
    for f in range(fields):
        turned = [turned_r[pl.ds((f * SUBS + g) * gap_w, cells_w), :] for g in range(SUBS)]
        turned_c[pl.ds(f * LANES, LANES), :] = jnp.concatenate(turned, axis=0).T

    loads[5].wait()

    def mix(q, carry):
        start = pl.multiple_of(q * 16, 16)
        xi = [turned_c[pl.ds(j * LANES + start, 16), :] for j in range(fields)]
        for k in range(fields):
            total = None
            for j in range(fields):
                term = coupling[pl.ds((k * fields + j) * LANES + start, 16), :].astype(jnp.float32) * xi[j]
                total = term if total is None else total + term
            for half_rows in range(16 // cells_n):
                mixed[pl.ds((k * LANES // cells_n + q * (16 // cells_n) + half_rows) * (cells_n + 1), cells_n), :] = (
                    total[half_rows * cells_n : (half_rows + 1) * cells_n]
                )
        return carry

    lax.fori_loop(0, LANES // 16, mix, 0, unroll=True)

    rhs, cells_eta_r = forward_rhs(cells_n, every(mixed, rows_eta, cells_n + 1), cells_eta, cell_store)
    for k, v in enumerate(rhs):
        put_parts(small_eta, k, lines, v)
    trees_eta_r = []
    for h in range(2):
        parts_r = [part() for part in packed(small_eta, lines, h * fields, 4)]
        whole_r, kept = tree_rhs(parts_r, trees_eta[h], small)
        for k, v in enumerate(whole_r):
            send_r[pl.ds(h * fields * 4 + k, fields, stride=4), :] = v
        trees_eta_r.append(kept)
    r_copies = to_homes(4, send_r, recv_r, send_r_sem, recv_r_sem)
    all_sent(me_n, m_copies)


    def each_home(act):
        for j, spot in enumerate(sites):

            @pl.when(my_spot == spot)
            def _():
                def one(o, carry):
                    act(home_copy(j, my_half * half + o + (o >= spot).astype(jnp.int32)))
                    return carry

                lax.fori_loop(0, half - 1, one, 0)

    @pl.when(own_eta)
    def _():
        await_rows(recv_m, (ring_n - 1) * 32, recv_m_sem)
        kept = Stash(stash_ring)

        def by_parity(ref, i, rows, count):
            slot = 2 * rows
            return [
                [ref[pl.ds(odd * slot + i * rows + k, ring_n // 2, stride=2 * slot), :] for k in range(count)]
                for odd in range(2)
            ]

        rings = [ring_matrix(*by_parity(recv_m, i, 16, 16), kept) for i in range(2)]
        await_rows(recv_r, (ring_n - 1) * 8, recv_r_sem)
        answers = [ring_rhs(*by_parity(recv_r, i, 4, 4), rings[i]) for i in range(2)]
        for i, answer in enumerate(answers):
            for k in range(4):
                for odd in range(2):
                    back_send_eta[pl.ds(odd * 8 + i * 4 + k, ring_n // 2, stride=16), :] = answer[odd][k]
        each_home(lambda copy: copy.start())
        for j, spot in enumerate(sites):

            @pl.when(my_spot == spot)
            def _():
                back_recv_eta[pl.ds(j * 8, 8), :] = back_send_eta[pl.ds(pl.multiple_of(me_n * 8, 8), 8), :]

    all_sent(me_n, r_copies)
    wait_back(lines * 4, own_eta, back_recv_eta, brecv_eta_sem)
    for h in range(2):
        joints = [back_recv_eta[pl.ds(h * fields * 4 + k, fields, stride=4), :] for k in range(4)]
        place_joints(tree_back(joints, trees_eta[h], trees_eta_r[h]), joints_eta, lines, h * fields)

    def write_eta(j, value):
        out_ref[pl.ds(j, rows_eta, stride=cells_n), :] = value

    back(
        cells_n, cells_eta, cells_eta_r,
        [get_parts(joints_eta, k, lines) for k in range(4)], write_eta,
    )

    def drain(size, src, send_sem, axis, me):
        def one(o, carry):
            d = o + (o >= me).astype(jnp.int32)
            slot = src.at[pl.ds(pl.multiple_of(d * 8, 8), 8), :]
            remote(slot, slot, send_sem.at[d], send_sem.at[d], axis, d).wait_send()
            return carry

        lax.fori_loop(0, size - 1, one, 0)

    @pl.when(own_xi)
    def _():
        drain(ring_w, back_send_xi, bsend_xi_sem, "wrap", me_w)

    @pl.when(own_eta)
    def _():
        each_home(lambda copy: copy.wait_send())


def solution(mesh):
    ring_w, ring_n = mesh.shape["wrap"], mesh.shape["normal"]

    def local(residual, courant_xi, courant_eta, dissip_xi, dissip_eta, coupling):
        fields, _, rows_n, _ = residual.shape
        lines = 2 * fields
        flat = fields * LANES
        cells_w, cells_n = LANES // SUBS, rows_n // SUBS
        xi_rows, eta_rows = fields * SUBS, lines * SUBS
        pad = -(-fields // 8) * 8
        _, sites = homes(lines, ring_n)
        vmem = lambda rows, dtype=jnp.float32: pltpu.VMEM((rows, LANES), dtype)
        dma = lambda count: pltpu.SemaphoreType.DMA((count,))
        scratch = [
            vmem(flat), vmem(flat), vmem(flat), vmem(LANES), vmem(LANES), vmem(fields * flat, jnp.bfloat16),
            vmem(flat + xi_rows), vmem(flat + xi_rows), vmem(LANES + SUBS), vmem(flat + eta_rows), vmem(20 * fields * (SUBS + 1)), vmem(16 * lines * (SUBS + 1)),
            vmem(fields * 24), vmem(ring_w * 24), vmem(ring_w * 8), vmem(fields * 8),
            vmem(lines * 16), vmem(ring_n * 32), vmem(lines * 4), vmem(ring_n * 8), vmem(ring_n * 8), vmem(lines * 4),
            vmem(4 * fields * (SUBS + 1)), vmem(4 * lines * (SUBS + 1)),
            vmem((cells_w - 2) * 5 * xi_rows + (cells_n - 2) * 10 * eta_rows),
            vmem((SUBS - 1) * 22 * 3 * pad),
            vmem(2 * (8 * 8 + 4 + 12) * max(8, ring_w // 2, ring_n // 2)),
            dma(6), dma(fields), pltpu.SemaphoreType.DMA, dma(ring_w), pltpu.SemaphoreType.DMA,
            dma(2 * len(sites)), pltpu.SemaphoreType.DMA, dma(2 * len(sites)), pltpu.SemaphoreType.DMA,
            dma(ring_n // 2), pltpu.SemaphoreType.DMA,
        ]
        out = pl.pallas_call(
            functools.partial(kernel, fields, ring_w, ring_n, rows_n),
            out_shape=jax.ShapeDtypeStruct((flat, LANES), jnp.float32),
            in_specs=[pl.BlockSpec(memory_space=pltpu.HBM)] * 6,
            out_specs=pl.BlockSpec(memory_space=pltpu.VMEM),
            scratch_shapes=scratch,
            compiler_params=pltpu.CompilerParams(
                collective_id=0, has_side_effects=True, vmem_limit_bytes=32 * 1024 * 1024
            ),
        )(
            *[pltpu.with_memory_space_constraint(v, pltpu.HBM) for v in (
            residual.reshape(flat, LANES), courant_xi.reshape(flat, LANES), courant_eta.reshape(flat, LANES),
            dissip_xi.reshape(LANES, LANES), dissip_eta.reshape(LANES, LANES), coupling.reshape(fields * flat, LANES),
            )]
        )
        return out.reshape(residual.shape)

    placed = (
        P(None, None, "normal", "wrap"),
        P(None, None, "normal", "wrap"),
        P(None, None, "normal", "wrap"),
        P(None, "normal", "wrap"),
        P(None, "normal", "wrap"),
        P(None, None, None, "normal", "wrap"),
    )
    return jax.shard_map(
        local, mesh=mesh, in_specs=placed, out_specs=P(None, None, "normal", "wrap"), check_vma=False
    )
```
